32 devices in a mesh: grp: 2 (over y), seq: 4 (over z), tp: 4 (over x, core).
Axes of the slice: x: 2, y: 2, z: 4, core: 2. Of those that a mesh axis runs over, the one named last changes fastest.
Arguments:
- ssm_input: bfloat16 [2048, 8192], P(('grp', 'seq'), 'tp'), parts along dimension 0, may hold values from -6 to 6
- bmat: bfloat16 [2048, 1024], P(('grp', 'seq'), 'tp'), parts along dimension 0, may hold values from -6 to 6
- cmat: bfloat16 [2048, 1024], P(('grp', 'seq'), 'tp'), parts along dimension 0, may hold values from -6 to 6
- dt_raw: bfloat16 [2048, 128], P(('grp', 'seq'), 'tp'), parts along dimension 0
- a_log: float32 [128], P('tp'), may hold values from -0.5 to 0.5
- d_skip: float32 [128], P('tp'), may hold values from 0.5 to 1.5
- prompt_len: int32 [16], P('grp'), parts along dimension 0, may hold values from 1 to 1024, as said below
- owner: int32 [16], P('grp'), parts along dimension 0, may hold values from 0 to 3, as said below
- dec_x: bfloat16 [8, 4, 4, 8192], P(('grp', 'seq'), None, None, 'tp'), parts along dimension 0, may hold values from -6 to 6
- dec_b: bfloat16 [8, 4, 4, 1024], P(('grp', 'seq'), None, None, 'tp'), parts along dimension 0, may hold values from -6 to 6
- dec_c: bfloat16 [8, 4, 4, 1024], P(('grp', 'seq'), None, None, 'tp'), parts along dimension 0, may hold values from -6 to 6
- dec_dt: bfloat16 [8, 4, 4, 128], P(('grp', 'seq'), None, None, 'tp'), parts along dimension 0
Outputs:
- prefill_out: bfloat16 [2048, 8192], P(('grp', 'seq'), 'tp'), parts along dimension 0
- decode_out: bfloat16 [8, 4, 4, 8192], P(('grp', 'seq'), None, None, 'tp'), parts along dimension 0
The draws below stay inside these ranges and needn't reach their ends.
There are 2 independent parts, one for each index of `grp`. The reference program is written for one: setup_inputs(seed, part) draws one part's arguments, and reference() takes and returns one part's arrays. A program takes and returns all parts, laid end to end along the dimension named above; an argument that names none is the same for every part. Nothing has to cross between parts.
Inputs may be any that keep to these rules, and one draw needn't show every extreme that they name: `prompt_len`: no two requests have both the same owner and the same 256-position part of the prompt holding their last prompt position. Each owner decodes at most 4 requests and each part holds the last position of at most 4; some owner and some part reach that in every draw. `owner`: every index of seq owns at least one request.
All inputs are finite; a program needn't handle non-finite values.
Results may differ from the reference program's by a relative error of at most 0.0055.
Values may be sent and summed in bfloat16 or wider, within the bound.
A program may use at most 128 MiB of HBM per device.

```python
import jax
import jax.numpy as jnp
from jax import lax

H = 128
P_SIZE = 64
N = 128
G = 8
SPAN = 128
STEPS = 4
SLICE_LENGTH = 256
INPUT_LENGTH = 1024
REQUEST_COUNT = 8
N_SEQ = 4


def head_levels(key, share_slow):
    kind_key = jax.random.fold_in(key, 101)
    level_key = jax.random.fold_in(key, 102)
    slow = jax.random.uniform(kind_key, (H,)) < share_slow
    spread = jax.random.uniform(level_key, (H,))
    slow_level = jnp.exp(jnp.log(0.1) + spread * (jnp.log(0.6) - jnp.log(0.1))) / SLICE_LENGTH
    fast_level = jnp.exp(jnp.log(1.0 / 50.0) + spread * (jnp.log(1.0 / 30.0) - jnp.log(1.0 / 50.0)))
    return jnp.where(slow, slow_level, fast_level)


def draw_dt_raw(key, part):
    share_slow = 0.5
    levels = head_levels(key, share_slow)
    block_key = jax.random.fold_in(key, 103)
    rough_key = jax.random.fold_in(key, 104)
    main_random_seed = jax.random.fold_in(key, 105)
    auxiliary_random_seed = jax.random.fold_in(key, 106)
    strength_key = jax.random.fold_in(key, 107)
    block_count = INPUT_LENGTH // SLICE_LENGTH
    factor = jnp.exp(jax.random.uniform(block_key, (block_count, H), minval=jnp.log(0.5), maxval=jnp.log(2.0)))
    factor = jnp.repeat(factor, SLICE_LENGTH, axis=0)
    noise = jax.random.truncated_normal(rough_key, -2.5, 2.5, (INPUT_LENGTH, H))
    destination_device = levels[None, :] * factor * jnp.exp(0.5 * noise)
    front_stretch = jax.random.randint(main_random_seed, (), 0, SLICE_LENGTH)
    closing_stretch = jax.random.randint(auxiliary_random_seed, (), SLICE_LENGTH, INPUT_LENGTH)
    assignment_table = jnp.arange(INPUT_LENGTH)
    input_stretch = (assignment_table == front_stretch) | (assignment_table == closing_stretch)
    magnitude_level = jax.random.uniform(strength_key, (INPUT_LENGTH, H), minval=0.2, maxval=0.5)
    destination_device = jnp.where(input_stretch[:, None], magnitude_level, destination_device)
    return jnp.log(jnp.expm1(destination_device)).astype(jnp.bfloat16)


def draw_dec_dt(key, part):
    share_slow = 0.5
    levels = head_levels(key, share_slow)
    rough_key = jax.random.fold_in(key, 108)
    noise = jax.random.truncated_normal(rough_key, -2.5, 2.5, (N_SEQ, N_SEQ, STEPS, H))
    destination_device = levels * jnp.exp(0.5 * noise)
    return jnp.log(jnp.expm1(destination_device)).astype(jnp.bfloat16)


def request_table(key):
    count = N_SEQ
    pairs = count * count
    owner_key = jax.random.fold_in(key, 201)
    source_key = jax.random.fold_in(key, 202)
    score_key = jax.random.fold_in(key, 203)
    offset_key = jax.random.fold_in(key, 204)
    complete_owner = jax.random.randint(owner_key, (), 0, count)
    complete_source = jax.random.randint(source_key, (), 0, count)
    numbers = jnp.arange(pairs, dtype=jnp.int32)
    row_lookup = numbers // count
    column_lookup = numbers % count
    score_values = jax.random.randint(score_key, (pairs,), 0, 2 ** 30 // pairs) * pairs + numbers
    extra_score = jnp.where((row_lookup == complete_owner) | (column_lookup == complete_source), 2 ** 30, 0)
    sorted_ranking, picked_heads = lax.top_k(score_values + extra_score, REQUEST_COUNT)
    owners = picked_heads // count
    sources = picked_heads % count
    offsets = jax.random.randint(offset_key, (REQUEST_COUNT,), 1, SLICE_LENGTH + 1)
    lengths = sources * SLICE_LENGTH + offsets
    return (owners.astype(jnp.int32), lengths.astype(jnp.int32))


def draw_prompt_len(key, part):
    return request_table(key)[1]


def draw_owner(key, part):
    return request_table(key)[0]


def shard_levels(stream_key, shape, split, low, largest):
    factor_of = 1.0
    for position, blocks in split:
        draws = jax.random.uniform(jax.random.fold_in(jax.random.fold_in(stream_key, 6), position), (blocks,), jnp.float32, low / len(split), largest / len(split))
        factor_of = factor_of * jnp.repeat(jnp.exp(draws), shape[position] // blocks).reshape((-1,) + (1,) * (len(shape) - 1 - position))
    return factor_of


def bell_draw(rng, extent, scale, most, shards=(), held_as=jnp.bfloat16):
    result = scale * jax.random.normal(rng, extent, jnp.float32)
    if shards:
        result = result * shard_levels(rng, extent, shards, -0.22, 0.18)
    return jnp.clip(result, -most, most).astype(held_as)


def setup_inputs(seed: int = 0, part: int = 0) -> dict:
    key_list = jax.random.split(jax.random.key(seed), 13)
    part_keys = jax.random.split(jax.random.fold_in(key_list[12], part), 13)
    return {
        "ssm_input": bell_draw(part_keys[0], (INPUT_LENGTH, H * P_SIZE), 1.0, 6.0, ((0, 4), (1, 4))),
        "bmat": bell_draw(part_keys[1], (INPUT_LENGTH, G * N), 1.0, 6.0, ((0, 4), (1, 4))),
        "cmat": bell_draw(part_keys[2], (INPUT_LENGTH, G * N), 1.0, 6.0, ((0, 4), (1, 4))),
        "dt_raw": draw_dt_raw(jax.random.fold_in(jax.random.fold_in(key_list[12], part), 71), part),
        "a_log": jnp.clip(jax.random.uniform(key_list[4], (H,), jnp.float32, -0.5, 0.5) * shard_levels(key_list[4], (H,), ((0, 4),), -0.4, 0.0), -0.5, 0.5),
        "d_skip": jnp.clip(0.5 + 1.0 * jax.random.uniform(key_list[5], (H,), jnp.float32) ** shard_levels(key_list[5], (H,), ((0, 4),), -0.2, 0.2), 0.5, 1.5),
        "prompt_len": draw_prompt_len(jax.random.fold_in(jax.random.fold_in(key_list[12], part), 71), part),
        "owner": draw_owner(jax.random.fold_in(jax.random.fold_in(key_list[12], part), 71), part),
        "dec_x": bell_draw(part_keys[8], (N_SEQ, N_SEQ, STEPS, H * P_SIZE), 1.0, 6.0, ((0, 4), (3, 4))),
        "dec_b": bell_draw(part_keys[9], (N_SEQ, N_SEQ, STEPS, G * N), 1.0, 6.0, ((0, 4), (3, 4))),
        "dec_c": bell_draw(part_keys[10], (N_SEQ, N_SEQ, STEPS, G * N), 1.0, 6.0, ((0, 4), (3, 4))),
        "dec_dt": draw_dec_dt(jax.random.fold_in(jax.random.fold_in(key_list[12], part), 71), part),
    }


def reference(ssm_input, bmat, cmat, dt_raw, a_log, d_skip, prompt_len, owner, dec_x, dec_b, dec_c, dec_dt):
    highest = lax.Precision.HIGHEST
    span_count = INPUT_LENGTH // SPAN
    per_group = H // G
    step_size = jax.nn.softplus(dt_raw.astype(jnp.float32))
    log_decay = -jnp.exp(a_log)[None, :] * step_size
    cumulative = jnp.cumsum(log_decay.reshape(span_count, SPAN, H), axis=1)
    step_spans = step_size.reshape(span_count, SPAN, H)
    x_spans = ssm_input.reshape(span_count, SPAN, H, P_SIZE)
    b_spans = bmat.reshape(span_count, SPAN, G, N)
    c_spans = cmat.reshape(span_count, SPAN, G, N)
    causal = jnp.arange(SPAN)[:, None] >= jnp.arange(SPAN)[None, :]

    def span_pass(state, items):
        x_part, b_part, c_part, cum_part, step_part = items
        score_values = jnp.einsum('tgn,sgn->gts', c_part.astype(jnp.float32), b_part.astype(jnp.float32), precision=highest)
        head_scores = jnp.repeat(score_values, per_group, axis=0)
        spread = cum_part.T[:, :, None] - cum_part.T[:, None, :]
        decay = jnp.where(causal[None], jnp.exp(jnp.where(causal[None], spread, 0.0)), 0.0)
        weights = (head_scores * decay * step_part.T[:, None, :]).astype(jnp.bfloat16)
        inner = jnp.einsum('hts,shp->thp', weights.astype(jnp.float32), x_part.astype(jnp.float32), precision=highest)
        b_heads = jnp.repeat(b_part, per_group, axis=1).astype(jnp.float32)
        scaled = (b_heads * (jnp.exp(cum_part[-1][None, :] - cum_part) * step_part)[:, :, None]).astype(jnp.bfloat16)
        span_state = jnp.einsum('shp,shn->hpn', x_part.astype(jnp.float32), scaled.astype(jnp.float32), precision=highest)
        carried = jnp.einsum('tgn,gjpn->tgjp', c_part.astype(jnp.float32), state.reshape(G, per_group, P_SIZE, N), precision=highest).reshape(SPAN, H, P_SIZE)
        outer = jnp.exp(cum_part)[:, :, None] * carried
        output = (inner + outer + d_skip[None, :, None] * x_part.astype(jnp.float32)).astype(jnp.bfloat16)
        following = jnp.exp(cum_part[-1])[:, None, None] * state + span_state
        return following, (output, state)

    initial = jnp.zeros((H, P_SIZE, N), jnp.float32)
    ending, (outputs, starts) = lax.scan(span_pass, initial, (x_spans, b_spans, c_spans, cumulative, step_spans))
    prefill_out = outputs.reshape(INPUT_LENGTH, H * P_SIZE)
    rate_scale = jnp.exp(a_log)
    positions = jnp.arange(SPAN)

    def request_pass(request):
        last_token = (prompt_len[request] - 1).astype(jnp.int32)
        span_index = (last_token // SPAN).astype(jnp.int32)
        offset = (last_token % SPAN).astype(jnp.int32)
        x_part = lax.dynamic_index_in_dim(x_spans, span_index, 0, keepdims=False)
        b_part = lax.dynamic_index_in_dim(b_spans, span_index, 0, keepdims=False)
        cum_part = lax.dynamic_index_in_dim(cumulative, span_index, 0, keepdims=False)
        step_part = lax.dynamic_index_in_dim(step_spans, span_index, 0, keepdims=False)
        state = lax.dynamic_index_in_dim(starts, span_index, 0, keepdims=False)
        cum_last = lax.dynamic_index_in_dim(cum_part, offset, 0, keepdims=False)
        upto = positions[:, None] <= offset
        weight = jnp.where(upto, jnp.exp(jnp.where(upto, cum_last[None, :] - cum_part, 0.0)) * step_part, 0.0)
        b_heads = jnp.repeat(b_part, per_group, axis=1).astype(jnp.float32)
        scaled = (b_heads * weight[:, :, None]).astype(jnp.bfloat16)
        local_sum = jnp.einsum('shp,shn->hpn', x_part.astype(jnp.float32), scaled.astype(jnp.float32), precision=highest)
        handed = (jnp.exp(cum_last)[:, None, None] * state + local_sum).astype(jnp.bfloat16)
        source = (last_token // SLICE_LENGTH).astype(jnp.int32)
        holder = owner[request].astype(jnp.int32)
        slot_x = dec_x[holder, source]
        slot_b = dec_b[holder, source]
        slot_c = dec_c[holder, source]
        slot_step = dec_dt[holder, source]
        hidden = handed.astype(jnp.float32)
        rows = []
        for turn in range(STEPS):
            step_now = jax.nn.softplus(slot_step[turn].astype(jnp.float32))
            x_now = slot_x[turn].reshape(H, P_SIZE).astype(jnp.float32)
            b_now = jnp.repeat(slot_b[turn].reshape(G, N), per_group, axis=0).astype(jnp.float32)
            c_now = jnp.repeat(slot_c[turn].reshape(G, N), per_group, axis=0).astype(jnp.float32)
            hidden = jnp.exp(-rate_scale * step_now)[:, None, None] * hidden + (step_now[:, None] * x_now)[:, :, None] * b_now[:, None, :]
            reading = jnp.einsum('hpn,hn->hp', hidden, c_now, precision=highest) + d_skip[:, None] * x_now
            rows.append(reading.reshape(H * P_SIZE))
        return jnp.stack(rows).astype(jnp.bfloat16)

    decoded = lax.map(request_pass, jnp.arange(REQUEST_COUNT, dtype=jnp.int32))
    sources = ((prompt_len - 1) // SLICE_LENGTH).astype(jnp.int32)
    decode_out = jnp.zeros((N_SEQ, N_SEQ, STEPS, H * P_SIZE), jnp.bfloat16).at[owner.astype(jnp.int32), sources].set(decoded)
    return (prefill_out, decode_out)
```

```python
import functools

import jax
import jax.numpy as jnp
from jax import lax
from jax.experimental import pallas as pl
from jax.experimental.pallas import tpu as pltpu
from jax.sharding import PartitionSpec as P

P_SIZE = 64
N = 128
SPAN = 128
STEPS = 4
LANES = 256
HOP = 128
PIECES = 2
MESH = pl.DeviceIdType.MESH
F32 = jnp.float32
BF16 = jnp.bfloat16
FAR = -1e30


def iota(shape, axis):
    return lax.broadcasted_iota(jnp.int32, shape, axis)


def dot(a, b):
    return jnp.dot(a, b, preferred_element_type=F32)


def dot_t(a, b):
    return lax.dot_general(a, b, (((1,), (1,)), ((), ())), preferred_element_type=F32)


def halves(value, count):
    pieces = []
    for _ in range(count):
        piece = value.astype(BF16)
        pieces.append(piece)
        value = value - piece.astype(F32)
    return pieces


def picked(selector, value, count=3):
    parts = [dot(selector, piece) for piece in halves(value, count)]
    return sum(parts[1:], parts[0])


def spread(pieces, expand):
    parts = [dot(piece, expand) for piece in pieces]
    return sum(parts[1:], parts[0])


def ones(mask):
    return jnp.where(mask, 1.0, 0.0).astype(BF16)


def softplus(value):
    return jnp.maximum(value, 0.0) + jnp.log1p(jnp.exp(-jnp.abs(value)))


def aligned(index):
    return index if isinstance(index, int) else pl.multiple_of(index, 8)


def each(count, body):
    if count <= 4:
        for i in range(count):
            body(i)
    else:

        def turn(i, carry):
            body(i)
            return carry

        lax.fori_loop(0, count, turn, 0)


def kernel(
    n,
    x_hbm, b_hbm, c_hbm, dt_hbm, alog_hbm, skip_hbm, len_hbm, own_hbm,
    dx_hbm, db_hbm, dc_hbm, ddt_hbm,
    out_ref, dout_ref,
    x_ref, b_ref, c_ref, dt_ref, alog_ref, skip_ref, len_ref, own_ref,
    dx_ref, db_ref, ddt_ref, queries,
    xd, bd, dtd, asked, asked_up, asked_own, asked_all,
    expand_ref, row_ref, first, total, base, inbuf, outbuf,
    res, local, reached, zbuf, zin, rbuf, rin, lgout, lgin, factor,
    load_sem, send_state, recv_state, send_query, recv_query,
    send_log, recv_log, send_z, recv_z, send_r, recv_r, here,
):
    me = lax.axis_index("seq")
    tokens, width = x_ref.shape
    heads = dt_ref.shape[0]
    groups = b_ref.shape[1] // N
    per_group = heads // groups
    spans = tokens // SPAN
    chunks = width // LANES
    heads_chunk = LANES // P_SIZE
    hops = width // HOP
    parts = LANES // HOP
    rows = n * STEPS
    middle = (me > 0) & (me < n - 1)
    ending = (me == 0) | (me == n - 1)

    def lanes(chunk):
        return slice(chunk * LANES, (chunk + 1) * LANES)

    barrier = pltpu.get_barrier_semaphore()

    def greet(q):
        @pl.when((q > me) | (q == me - 1))
        def _():
            pl.semaphore_signal(barrier, inc=1, device_id={"seq": q}, device_id_type=MESH)

    sources = [
        (dt_hbm, dt_ref),
        (alog_hbm, alog_ref),
        (b_hbm, b_ref),
    ]
    cuts = [0, LANES, 2 * LANES, 4 * LANES, width]
    for begin, end in zip(cuts[:-1], cuts[1:]):
        sources.append((x_hbm.at[:, begin:end], x_ref.at[:, begin:end]))
    sources += [
        (c_hbm, c_ref),
        (dc_hbm.at[0], queries.at[me]),
        (skip_hbm, skip_ref),
        (len_hbm, len_ref),
        (own_hbm, own_ref),
        (ddt_hbm.at[0], ddt_ref),
        (db_hbm.at[0], db_ref),
        (dx_hbm.at[0], dx_ref),
    ]
    loads = [
        pltpu.make_async_copy(source, landing, load_sem.at[k])
        for k, (source, landing) in enumerate(sources)
    ]
    for copy in loads:
        copy.start()
    each(n, greet)

    def push(source, landing, sends, recvs, target):
        return pltpu.make_async_remote_copy(
            src_ref=source, dst_ref=landing, send_sem=sends, recv_sem=recvs,
            device_id={"seq": target}, device_id_type=MESH,
        )

    def query(q, origin):
        return push(
            queries.at[origin], queries.at[origin], send_query.at[q], recv_query.at[origin], q
        )

    def log_to(q, origin):
        return push(lgout.at[q], lgin.at[origin], send_log.at[q], recv_log.at[origin], q)

    def z_to(q, origin):
        return push(zbuf.at[q], zin.at[origin], send_z.at[q], recv_z.at[origin], q)

    def r_to(q, origin, piece):
        return push(
            rbuf.at[piece, q], rin.at[piece, origin],
            send_r.at[piece, q], recv_r.at[piece, origin], q,
        )

    def onward(hop):
        return push(
            outbuf.at[hop], inbuf.at[hop], send_state.at[hop], recv_state.at[hop],
            lax.rem(me + 1, n),
        )

    expand_ref[...] = ones(iota((heads, width), 0) == iota((heads, width), 1) // P_SIZE)
    t_row, t_col = iota((tokens, tokens), 0), iota((tokens, tokens), 1)
    upper = ones(((t_row // SPAN) == (t_col // SPAN)) & (t_col <= t_row))
    loads[0].wait()
    loads[1].wait()
    step_t = softplus(dt_ref[...].astype(F32))
    step = step_t.T
    rate = -jnp.exp(alog_ref[...])
    cum = picked(upper, rate * step)
    last = [cum[(s + 1) * SPAN - 1:(s + 1) * SPAN, :] for s in range(spans)]
    whole = sum(last[1:], last[0])
    into = jnp.concatenate(
        [
            jnp.exp(last[s] - cum[s * SPAN:(s + 1) * SPAN]) * step[s * SPAN:(s + 1) * SPAN]
            for s in range(spans)
        ],
        axis=0,
    )
    into_parts = halves(into, 2)
    grown = [halves(jnp.exp(last[s]), 2) for s in range(spans)]
    loads[2].wait()
    b_t = [
        [b_ref[s * SPAN:(s + 1) * SPAN, g * N:(g + 1) * N].T for g in range(groups)]
        for s in range(spans)
    ]

    def entered():
        pl.semaphore_wait(barrier, me + jnp.where(me < n - 1, 1, 0))

    for chunk in range(chunks):
        if chunk * LANES in cuts:
            loads[3 + cuts.index(chunk * LANES)].wait()
        g = chunk * heads_chunk // per_group
        expand = expand_ref[:, lanes(chunk)]
        weighted = (x_ref[:, lanes(chunk)].astype(F32) * spread(into_parts, expand)).astype(BF16)
        state = None
        for s in range(spans):
            own = dot(b_t[s][g], weighted[s * SPAN:(s + 1) * SPAN])
            state = own if state is None else spread(grown[s], expand) * state + own
            if s < spans - 1:
                first[s, :, lanes(chunk)] = state
        total[:, lanes(chunk)] = state
        if chunk == 0:
            entered()

        @pl.when(me == 0)
        def _():
            for part in range(parts):
                hop = chunk * parts + part
                outbuf[hop] = state[:, part * HOP:(part + 1) * HOP].astype(BF16)
                onward(hop).start()
                inbuf[hop] = jnp.zeros(inbuf.shape[1:], BF16)

        if chunk == 0:

            def announce(q):
                @pl.when(q < me - 1)
                def _():
                    pl.semaphore_signal(here, inc=1, device_id={"seq": q}, device_id_type=MESH)

            each(n, announce)
        if chunk == 3:
            k = 3 + len(cuts) - 1
            for copy in loads[k:]:
                copy.wait()

            def ask_near(q):
                @pl.when((q < me) | (q == me + 1))
                def _():
                    query(q, me).start()

            each(n, ask_near)

    @pl.when(me < n - 2)
    def _():
        pl.semaphore_wait(here, n - 2 - me)

    def ask_far(q):
        @pl.when(q > me + 1)
        def _():
            query(q, me).start()

    each(n, ask_far)

    outer_parts = halves(jnp.exp(cum), 2)
    cum_t = cum.T
    row_kind = iota((8, heads), 0)
    row_value = jnp.where(
        row_kind == 0, jnp.exp(whole), jnp.where(row_kind == 1, skip_ref[...], jnp.exp(last[0]))
    )
    row_ref[...] = spread(halves(row_value, 3), expand_ref[...])

    scores = []
    for s in range(spans):
        at = slice(s * SPAN, (s + 1) * SPAN)
        scores.append([])
        for g in range(groups):
            cols = slice(g * N, (g + 1) * N)
            scores[s].append(dot_t(c_ref[at, cols], b_ref[at, cols]))
    causal = iota((SPAN, SPAN), 0) >= iota((SPAN, SPAN), 1)
    low = ones(iota((1, 2 * P_SIZE), 1) < P_SIZE)
    high = ones(iota((1, 2 * P_SIZE), 1) >= P_SIZE)

    def pair_input(start, s):
        x_pair = x_ref[s * SPAN:(s + 1) * SPAN, start:start + 2 * P_SIZE]
        return jnp.concatenate([x_pair * low, x_pair * high], axis=0)

    def weights(head, s):
        at = slice(s * SPAN, (s + 1) * SPAN)
        gap = jnp.where(causal, cum[at, head:head + 1] - cum_t[head:head + 1, at], FAR)
        main = scores[s][head // per_group] * jnp.exp(gap) * step_t[head:head + 1, at]
        return main.astype(BF16)

    def inner(hop):
        head, start = hop * HOP // P_SIZE, hop * HOP
        for s in range(spans):
            at = slice(s * SPAN, (s + 1) * SPAN)
            left = jnp.concatenate([weights(head, s), weights(head + 1, s)], axis=1)
            skipped = row_ref[1:2, start:start + HOP] * x_ref[at, start:start + HOP].astype(F32)
            base[at, start:start + HOP] = dot(left, pair_input(start, s)) + skipped

    def relay(hop):
        @pl.when(middle)
        def _():
            onward(hop).wait_recv()
            at = slice(hop * HOP, (hop + 1) * HOP)
            outbuf[hop] = (row_ref[0:1, at] * inbuf[hop].astype(F32) + total[:, at]).astype(BF16)
            onward(hop).start()

    asked_up[...] = jnp.zeros(asked_up.shape, F32)

    def asked_from_above():
        for q in range(n):

            @pl.when(q > me)
            def _():
                query(me, q).wait_recv()
                asked_up[q * STEPS:(q + 1) * STEPS, :] = queries[q, me].astype(F32)


    def asked_from_below():
        def take(q):
            @pl.when(q < me)
            def _():
                query(me, q).wait_recv()

        each(n, take)
        for s in range(n):
            asked[s * STEPS:(s + 1) * STEPS, :] = queries[s, me].astype(F32)

        def lay(q):
            found = jnp.concatenate([queries[q, s].astype(F32) for s in range(n)], axis=0)
            asked_all[pl.ds(aligned(q * rows), rows), :] = found

        each(n, lay)

    for s in range(n):
        asked_own[s * STEPS:(s + 1) * STEPS, :] = queries[me, s].astype(F32)
        xd[s * STEPS:(s + 1) * STEPS, :] = dx_ref[s].astype(F32)
        bd[s * STEPS:(s + 1) * STEPS, :] = db_ref[s].astype(F32)
        dtd[s * STEPS:(s + 1) * STEPS, :] = ddt_ref[s].astype(F32)

    requests = len_ref.shape[1]
    final = len_ref[...] - 1
    row_r = iota((rows, requests), 0) // STEPS
    here_now = (final >= me * tokens) & (final < (me + 1) * tokens)
    chosen = here_now & (own_ref[...] == row_r)
    spot = jnp.sum(jnp.where(chosen, final - me * tokens, 0), axis=1, keepdims=True)
    place = iota((rows, tokens), 1)
    upto = (place <= spot) & (place // SPAN == spot // SPAN)
    cum_spot = picked(ones(place == spot), cum)
    spot_span = spot // SPAN
    spot_parts = halves(jnp.exp(cum_spot), 2)
    reach = cum_spot
    for s in range(spans - 1):
        reach = reach + jnp.where(spot_span > s, last[s], 0.0)
    reach_parts = halves(jnp.exp(reach), 2)
    for q in range(n):
        lgout[q] = jnp.where(row_kind == 0, reach[q * STEPS:q * STEPS + 1], whole)

    def tell(q):
        @pl.when(q < me)
        def _():
            log_to(q, me).start()

    each(n, tell)

    wanted = (
        (own_ref[...] == me) & (final >= row_r * tokens) & (final < (row_r + 1) * tokens)
    )
    present = jnp.sum(jnp.where(wanted, 1, 0), axis=1, keepdims=True) > 0
    r_row, r_col = iota((rows, rows), 0), iota((rows, rows), 1)
    slot = (r_row // STEPS) == (r_col // STEPS)
    row_h = iota((rows, heads), 0)

    def owner_start():
        dstep = softplus(dtd[...])
        running = picked(ones(slot & (r_col <= r_row)), rate * dstep)
        c_own = asked_own[...].astype(BF16)
        b_own = bd[...].astype(BF16)
        head_group = iota((rows, heads), 1) // per_group
        pairs = [
            dot_t(c_own[:, g * N:(g + 1) * N], b_own[:, g * N:(g + 1) * N]) for g in range(groups)
        ]
        fresh_parts, fresh_pick = [], []
        for k in range(STEPS):
            chosen_k = slot & (r_col % STEPS == k)
            pick = ones(chosen_k)
            score = jnp.zeros((rows, heads), F32)
            for g in range(groups):
                value = jnp.sum(jnp.where(chosen_k, pairs[g], 0.0), axis=1, keepdims=True)
                score = jnp.where(head_group == g, value, score)
            gap = jnp.where(row_h % STEPS >= k, running - picked(pick, running), FAR)
            fresh_parts.append(halves(jnp.exp(gap) * picked(pick, dstep) * score, 2))
            fresh_pick.append(pick)
        for chunk in range(chunks):
            expand = expand_ref[:, lanes(chunk)]
            xd_part = xd[:, lanes(chunk)]
            value = row_ref[1:2, lanes(chunk)] * xd_part
            for k in range(STEPS):
                value = value + spread(fresh_parts[k], expand) * dot(
                    fresh_pick[k], xd_part.astype(BF16)
                )
            res[:, lanes(chunk)] = value
        return running

    def owner_factors(running):
        def heard(q):
            @pl.when(q > me)
            def _():
                log_to(me, q).wait_recv()

        each(n, heard)
        row_s = row_h // STEPS
        exponent = reach
        for s in range(n):
            exponent = jnp.where((row_s == s) & (s > me), lgin[s, 0:1, :], exponent)
        for q in reversed(range(n)):
            level = jnp.where(row_s > q, exponent, jnp.where(row_s == q, 0.0, FAR))
            for k, piece in enumerate(halves(jnp.exp(running + level), 2)):
                factor[q, k] = piece
            through = jnp.where(q > me, lgin[q, 1:2, :], jnp.where(q == me, whole, 0.0))
            exponent = exponent + jnp.where(row_s > q, through, 0.0)
        level = jnp.where(row_s > me, exponent, jnp.where(row_s == me, reach, FAR))
        for k, piece in enumerate(halves(jnp.exp(running + level), 2)):
            factor[n, k] = piece
        for k, piece in enumerate(halves(jnp.exp(running), 2)):
            factor[n + 1, k] = piece

    def scale(index, chunk):
        expand = expand_ref[:, lanes(chunk)]
        return dot(factor[index, 0], expand) + dot(factor[index, 1], expand)

    def source_scores():
        found = asked[...].astype(BF16)
        return [
            [
                dot_t(found[:, g * N:(g + 1) * N], b_ref[s * SPAN:(s + 1) * SPAN, g * N:(g + 1) * N])
                for g in range(groups)
            ]
            for s in range(spans)
        ]

    def source_part(chunk, dec_scores):
        g = chunk * heads_chunk // per_group
        cols = slice(g * N, (g + 1) * N)
        found = asked[:, cols].astype(BF16)
        expand = expand_ref[:, lanes(chunk)]
        side = []
        for part in range(parts):
            hop = chunk * parts + part
            head, start = hop * HOP // P_SIZE, hop * HOP
            value = None
            for s in range(spans):
                at = slice(s * SPAN, (s + 1) * SPAN)
                left = []
                for h in (head, head + 1):
                    gap = jnp.where(upto[:, at], cum_spot[:, h:h + 1] - cum_t[h:h + 1, at], FAR)
                    left.append(
                        (dec_scores[s][g] * jnp.exp(gap) * step_t[h:h + 1, at]).astype(BF16)
                    )
                more = dot(jnp.concatenate(left, axis=1), pair_input(start, s))
                value = more if value is None else value + more
            side.append(value)
        value = jnp.concatenate(side, axis=1)
        held = jnp.zeros((rows, LANES), F32)
        for s in range(1, spans):
            begun = dot(found, first[s - 1, :, lanes(chunk)].astype(BF16))
            held = jnp.where(spot_span == s, begun, held)
        value = value + spread(spot_parts, expand) * held
        local[:, lanes(chunk)] = value
        state = total[:, lanes(chunk)].astype(BF16)
        if n <= 4:
            everything = dot(asked_all[:, cols].astype(BF16), state)

        def lay(i):
            local_i = local[pl.ds(aligned(i * 2 * STEPS), 2 * STEPS), lanes(chunk)]
            for half in range(2):
                q = 2 * i + half
                if n <= 4:
                    found_q = everything[q * rows:(q + 1) * rows]
                else:
                    left = asked_all[pl.ds(aligned(q * rows), rows), cols]
                    found_q = dot(left.astype(BF16), state)
                for s in range(n):
                    zbuf[q, s, :, lanes(chunk)] = jnp.where(
                        me == s,
                        local_i[half * STEPS:(half + 1) * STEPS],
                        found_q[s * STEPS:(s + 1) * STEPS],
                    ).astype(BF16)

        each(n // 2, lay)

    def add_z(ref, q, chunk):
        value = jnp.concatenate([ref[q, s, :, lanes(chunk)].astype(F32) for s in range(n)], axis=0)
        res[:, lanes(chunk)] += scale(q, chunk) * value

    def carry(chunk):
        g = chunk * heads_chunk // per_group
        cols = slice(g * N, (g + 1) * N)
        expand = expand_ref[:, lanes(chunk)]
        outer = spread(outer_parts, expand)
        incoming = jnp.concatenate([inbuf[chunk * parts + p] for p in range(parts)], axis=1)
        for s in range(spans):
            at = slice(s * SPAN, (s + 1) * SPAN)
            if s == 0:
                left = jnp.concatenate(
                    [
                        c_ref[at, cols],
                        asked_up[:, cols].astype(BF16),
                        asked_own[:, cols].astype(BF16),
                    ],
                    axis=0,
                )
                held = incoming
                passed = None
            else:
                left = c_ref[at, cols]
                step_on = row_ref[2:3, lanes(chunk)] if s == 1 else spread(grown[s - 1], expand)
                passed = step_on if passed is None else passed * step_on
                held = (
                    passed * incoming.astype(F32) + first[s - 1, :, lanes(chunk)]
                ).astype(BF16)
            carried = dot(left, held)
            out_ref[at, lanes(chunk)] = (
                base[at, lanes(chunk)] + outer[at] * carried[:SPAN]
            ).astype(BF16)
            if s == 0:
                reached[:, lanes(chunk)] = (
                    spread(reach_parts, expand) * carried[SPAN:SPAN + rows]
                )
                gathered[:, lanes(chunk)] = carried[SPAN + rows:]

    gathered = xd

    def give(piece):
        wide = width // PIECES
        area = slice(piece * wide, (piece + 1) * wide)
        value = (reached[:, area] + local[:, area]).astype(BF16)
        for q in range(n):
            rbuf[piece, q] = value[q * STEPS:(q + 1) * STEPS]

        def hand(q):
            @pl.when(q > me)
            def _():
                r_to(q, me, piece).start()

        each(n, hand)

    running = None
    dec_scores = None
    for chunk in range(chunks):
        for part in range(parts):
            inner(chunk * parts + part)
            relay(chunk * parts + part)
        if chunk == 0:
            running = owner_start()

            @pl.when(middle)
            def _():
                asked_from_above()

        @pl.when(middle)
        def _():
            carry(chunk)

        if chunk == 1:

            @pl.when(ending)
            def _():
                asked_from_above()

            asked_from_below()
            dec_scores = source_scores()
        if 2 <= chunk < 6:
            for more in range((chunk - 2) * chunks // 4, (chunk - 1) * chunks // 4):
                source_part(more, dec_scores)
        if chunk == 5:

            def answer(q):
                @pl.when(q < me)
                def _():
                    z_to(q, me).start()

            each(n, answer)
            owner_factors(running)
        if chunk == 6:
            for more in range(chunks):
                add_z(zbuf, me, more)

            @pl.when(middle)
            def _():
                give(0)

    @pl.when(me == n - 1)
    def _():
        for chunk in range(chunks):
            for part in range(parts):
                onward(chunk * parts + part).wait_recv()
            carry(chunk)

    @pl.when(me == 0)
    def _():
        for chunk in range(chunks):
            carry(chunk)
        give(0)

    @pl.when(me < n - 1)
    def _():
        give(1)

    for chunk in range(chunks):
        res[:, lanes(chunk)] += scale(n, chunk) * gathered[:, lanes(chunk)]

    def collect(q):
        @pl.when(q > me)
        def _():
            z_to(me, q).wait_recv()
            for chunk in range(chunks):
                add_z(zin, q, chunk)

    each(n, collect)

    def receive(q):
        @pl.when(q < me)
        def _():
            for piece in range(PIECES):
                r_to(me, q, piece).wait_recv()
            wide = width // PIECES
            for chunk in range(chunks):
                at = chunk * LANES % wide
                value = rin[chunk * LANES // wide, q, :, at:at + LANES].astype(F32)
                grow = dot(running_rows[0], expand_ref[:, lanes(chunk)]) + dot(
                    running_rows[1], expand_ref[:, lanes(chunk)]
                )
                kept = jnp.where(iota((rows, 1), 0) // STEPS == q, grow, 0.0)
                tall = jnp.concatenate([value] * n, axis=0)
                res[:, lanes(chunk)] += kept * tall

    running_rows = [factor[n + 1, 0], factor[n + 1, 1]]
    each(n, receive)
    done = jnp.where(present, res[...], 0.0).astype(BF16)
    for s in range(n):
        dout_ref[0, s] = done[s * STEPS:(s + 1) * STEPS]

    @pl.when(me < n - 1)
    def _():
        for hop in range(hops):
            onward(hop).wait_send()

    def finish(q):
        @pl.when(q != me)
        def _():
            query(q, me).wait_send()

        @pl.when(q < me)
        def _():
            log_to(q, me).wait_send()
            z_to(q, me).wait_send()

        @pl.when(q > me)
        def _():
            for piece in range(PIECES):
                r_to(q, me, piece).wait_send()

    each(n, finish)


def store(out_vmem, dout_vmem, out_hbm, dout_hbm, sem):
    copies = [
        pltpu.make_async_copy(out_vmem, out_hbm, sem.at[0]),
        pltpu.make_async_copy(dout_vmem, dout_hbm, sem.at[1]),
    ]
    for copy in copies:
        copy.start()
    for copy in copies:
        copy.wait()


def shards(
    ssm_input, bmat, cmat, dt_raw, a_log, d_skip, prompt_len, owner, dec_x, dec_b, dec_c, dec_dt
):
    n = lax.axis_size("seq")
    tokens, width = ssm_input.shape
    heads = dt_raw.shape[1]
    gn = bmat.shape[1]
    spans = tokens // SPAN
    hops = width // HOP
    rows = n * STEPS
    requests = prompt_len.shape[0]
    hbm = pl.BlockSpec(memory_space=pltpu.HBM)
    vmem = pl.BlockSpec(memory_space=pltpu.VMEM)
    dma = pltpu.SemaphoreType.DMA
    slots = (n, STEPS)
    operands = (
        ssm_input, bmat, cmat, dt_raw.T, a_log[None, :], d_skip[None, :],
        prompt_len[None, :], owner[None, :], dec_x, dec_b, dec_c, dec_dt,
    )
    out, dout = pl.pallas_call(
        functools.partial(kernel, n),
        out_shape=(
            pltpu.VMEM((tokens, width), BF16),
            pltpu.VMEM((1,) + slots + (width,), BF16),
        ),
        in_specs=[hbm] * 12,
        out_specs=(vmem, vmem),
        scratch_shapes=[
            pltpu.VMEM((tokens, width), BF16),
            pltpu.VMEM((tokens, gn), BF16),
            pltpu.VMEM((tokens, gn), BF16),
            pltpu.VMEM((heads, tokens), BF16),
            pltpu.VMEM((1, heads), F32),
            pltpu.VMEM((1, heads), F32),
            pltpu.VMEM((1, requests), jnp.int32),
            pltpu.VMEM((1, requests), jnp.int32),
            pltpu.VMEM(slots + (width,), BF16),
            pltpu.VMEM(slots + (gn,), BF16),
            pltpu.VMEM(slots + (heads,), BF16),
            pltpu.VMEM((n,) + slots + (gn,), BF16),
            pltpu.VMEM((rows, width), F32),
            pltpu.VMEM((rows, gn), F32),
            pltpu.VMEM((rows, heads), F32),
            pltpu.VMEM((rows, gn), F32),
            pltpu.VMEM((rows, gn), F32),
            pltpu.VMEM((rows, gn), F32),
            pltpu.VMEM((n * rows, gn), F32),
            pltpu.VMEM((heads, width), BF16),
            pltpu.VMEM((8, width), F32),
            pltpu.VMEM((max(spans - 1, 1), N, width), F32),
            pltpu.VMEM((N, width), F32),
            pltpu.VMEM((tokens, width), F32),
            pltpu.VMEM((hops, N, HOP), BF16),
            pltpu.VMEM((hops, N, HOP), BF16),
            pltpu.VMEM((rows, width), F32),
            pltpu.VMEM((rows, width), F32),
            pltpu.VMEM((rows, width), F32),
            pltpu.VMEM((n,) + slots + (width,), BF16),
            pltpu.VMEM((n,) + slots + (width,), BF16),
            pltpu.VMEM((PIECES, n, STEPS, width // PIECES), BF16),
            pltpu.VMEM((PIECES, n, STEPS, width // PIECES), BF16),
            pltpu.VMEM((n, 8, heads), F32),
            pltpu.VMEM((n, 8, heads), F32),
            pltpu.VMEM((n + 2, 2, rows, heads), BF16),
            dma((15,)),
            dma((hops,)),
            dma((hops,)),
            dma((n,)),
            dma((n,)),
            dma((n,)),
            dma((n,)),
            dma((n,)),
            dma((n,)),
            dma((PIECES, n)),
            dma((PIECES, n)),
            pltpu.SemaphoreType.REGULAR,
        ],
        compiler_params=pltpu.CompilerParams(
            collective_id=0, has_side_effects=True, vmem_limit_bytes=56 * 1024 * 1024
        ),
    )(*(pltpu.with_memory_space_constraint(operand, pltpu.HBM) for operand in operands))
    return pl.pallas_call(
        store,
        out_shape=(
            jax.ShapeDtypeStruct(out.shape, BF16),
            jax.ShapeDtypeStruct(dout.shape, BF16),
        ),
        in_specs=[vmem, vmem],
        out_specs=(hbm, hbm),
        scratch_shapes=[dma((2,))],
    )(
        pltpu.with_memory_space_constraint(out, pltpu.VMEM),
        pltpu.with_memory_space_constraint(dout, pltpu.VMEM),
    )


def solution(mesh):
    placed = (
        P(("grp", "seq"), "tp"),
        P(("grp", "seq"), "tp"),
        P(("grp", "seq"), "tp"),
        P(("grp", "seq"), "tp"),
        P("tp"),
        P("tp"),
        P("grp"),
        P("grp"),
        P(("grp", "seq"), None, None, "tp"),
        P(("grp", "seq"), None, None, "tp"),
        P(("grp", "seq"), None, None, "tp"),
        P(("grp", "seq"), None, None, "tp"),
    )
    return jax.shard_map(
        shards,
        mesh=mesh,
        in_specs=placed,
        out_specs=(P(("grp", "seq"), "tp"), P(("grp", "seq"), None, None, "tp")),
        check_vma=False,
    )
```

```python
import functools

import jax
import jax.numpy as jnp
from jax import lax
from jax.experimental import pallas as pl
from jax.experimental.pallas import tpu as pltpu
from jax.sharding import PartitionSpec as P

P_SIZE = 64
N = 128
SPAN = 128
STEPS = 4
LANES = 256
HOP = 128
PIECES = 2
EARLY = 4
MESH = pl.DeviceIdType.MESH
F32 = jnp.float32
BF16 = jnp.bfloat16
FAR = -1e30


def iota(shape, axis):
    return lax.broadcasted_iota(jnp.int32, shape, axis)


def dot(a, b):
    return jnp.dot(a, b, preferred_element_type=F32)


def dot_t(a, b):
    return lax.dot_general(a, b, (((1,), (1,)), ((), ())), preferred_element_type=F32)


def halves(value, count):
    pieces = []
    for _ in range(count):
        piece = value.astype(BF16)
        pieces.append(piece)
        value = value - piece.astype(F32)
    return pieces


def picked(selector, value, count=3):
    parts = [dot(selector, piece) for piece in halves(value, count)]
    return sum(parts[1:], parts[0])


def spread(pieces, expand):
    parts = [dot(piece, expand) for piece in pieces]
    return sum(parts[1:], parts[0])


def ones(mask):
    return jnp.where(mask, 1.0, 0.0).astype(BF16)


def softplus(value):
    return jnp.maximum(value, 0.0) + jnp.log1p(jnp.exp(-jnp.abs(value)))


def aligned(index):
    return index if isinstance(index, int) else pl.multiple_of(index, 8)


def each(count, body):
    if count <= 4:
        for i in range(count):
            body(i)
    else:

        def turn(i, carry):
            body(i)
            return carry

        lax.fori_loop(0, count, turn, 0)


def kernel(
    n,
    x_hbm, b_hbm, c_hbm, dt_hbm, alog_hbm, skip_hbm, len_hbm, own_hbm,
    dx_hbm, db_hbm, dc_hbm, ddt_hbm,
    out_ref, dout_ref,
    x_ref, b_ref, c_ref, dt_ref, alog_ref, skip_ref, len_ref, own_ref,
    dx_ref, db_ref, ddt_ref, queries,
    xd, bd, dtd, asked, asked_own, asked_all,
    expand_ref, row_ref, first, total, base, inbuf, outbuf,
    res, local, reached, zbuf, zin, rbuf, rin, lgout, lgin, factor,
    load_sem, send_state, recv_state, send_query, recv_query,
    send_log, recv_log, send_z, recv_z, send_r, recv_r, here,
):
    me = lax.axis_index("seq")
    tokens, width = x_ref.shape
    heads = dt_ref.shape[0]
    groups = b_ref.shape[1] // N
    per_group = heads // groups
    spans = tokens // SPAN
    chunks = width // LANES
    heads_chunk = LANES // P_SIZE
    hops = width // HOP
    parts = LANES // HOP
    rows = n * STEPS
    middle = (me > 0) & (me < n - 1)
    ending = (me == 0) | (me == n - 1)

    def lanes(chunk):
        return slice(chunk * LANES, (chunk + 1) * LANES)

    barrier = pltpu.get_barrier_semaphore()

    def greet(q):
        @pl.when((q > me) | (q == me - 1))
        def _():
            pl.semaphore_signal(barrier, inc=1, device_id={"seq": q}, device_id_type=MESH)

    sources = [
        (dt_hbm, dt_ref),
        (alog_hbm, alog_ref),
        (b_hbm, b_ref),
        (dc_hbm.at[0], queries.at[me]),
    ]
    cuts = [0, LANES, 2 * LANES, 4 * LANES, width]
    for begin, end in zip(cuts[:-1], cuts[1:]):
        sources.append((x_hbm.at[:, begin:end], x_ref.at[:, begin:end]))
    sources += [
        (c_hbm, c_ref),
        (skip_hbm, skip_ref),
        (len_hbm, len_ref),
        (own_hbm, own_ref),
        (ddt_hbm.at[0], ddt_ref),
        (db_hbm.at[0], db_ref),
        (dx_hbm.at[0], dx_ref),
    ]
    loads = [
        pltpu.make_async_copy(source, landing, load_sem.at[k])
        for k, (source, landing) in enumerate(sources)
    ]
    for copy in loads:
        copy.start()
    each(n, greet)

    def push(source, landing, sends, recvs, target):
        return pltpu.make_async_remote_copy(
            src_ref=source, dst_ref=landing, send_sem=sends, recv_sem=recvs,
            device_id={"seq": target}, device_id_type=MESH,
        )

    def query(q, origin):
        return push(
            queries.at[origin], queries.at[origin], send_query.at[q], recv_query.at[origin], q
        )

    def log_to(q, origin):
        return push(lgout.at[q], lgin.at[origin], send_log.at[q], recv_log.at[origin], q)

    def z_to(q, origin, s):
        return push(
            zbuf.at[q, s], zin.at[origin, s], send_z.at[q, s], recv_z.at[origin, s], q
        )

    def slots_from(origin, body):
        def turn(s):
            @pl.when(s >= origin)
            def _():
                body(s)

        each(n, turn)

    def r_to(q, origin, piece):
        return push(
            rbuf.at[piece, q], rin.at[piece, origin],
            send_r.at[piece, q], recv_r.at[piece, origin], q,
        )

    def onward(hop):
        return push(
            outbuf.at[hop], inbuf.at[hop], send_state.at[hop], recv_state.at[hop],
            lax.rem(me + 1, n),
        )

    def entered():
        pl.semaphore_wait(barrier, me + jnp.where(me < n - 1, 1, 0))

    @pl.when(me >= 2)
    def _():
        entered()

        def announce(q):
            @pl.when(q < me - 1)
            def _():
                pl.semaphore_signal(here.at[me], inc=1, device_id={"seq": q}, device_id_type=MESH)

        each(n, announce)

    expand_ref[...] = ones(iota((heads, width), 0) == iota((heads, width), 1) // P_SIZE)
    t_row, t_col = iota((tokens, tokens), 0), iota((tokens, tokens), 1)
    upper = ones(((t_row // SPAN) == (t_col // SPAN)) & (t_col <= t_row))
    loads[0].wait()
    loads[1].wait()
    step_t = softplus(dt_ref[...].astype(F32))
    step = step_t.T
    rate = -jnp.exp(alog_ref[...])
    cum = picked(upper, rate * step)
    last = [cum[(s + 1) * SPAN - 1:(s + 1) * SPAN, :] for s in range(spans)]
    whole = sum(last[1:], last[0])
    into = jnp.concatenate(
        [
            jnp.exp(last[s] - cum[s * SPAN:(s + 1) * SPAN]) * step[s * SPAN:(s + 1) * SPAN]
            for s in range(spans)
        ],
        axis=0,
    )
    into_parts = halves(into, 2)
    grown = [halves(jnp.exp(last[s]), 2) for s in range(spans)]
    loads[2].wait()
    b_t = [
        [b_ref[s * SPAN:(s + 1) * SPAN, g * N:(g + 1) * N].T for g in range(groups)]
        for s in range(spans)
    ]

    for chunk in range(chunks):
        if chunk * LANES in cuts:
            loads[4 + cuts.index(chunk * LANES)].wait()
        g = chunk * heads_chunk // per_group
        expand = expand_ref[:, lanes(chunk)]
        weighted = (x_ref[:, lanes(chunk)].astype(F32) * spread(into_parts, expand)).astype(BF16)
        state = None
        for s in range(spans):
            own = dot(b_t[s][g], weighted[s * SPAN:(s + 1) * SPAN])
            state = own if state is None else spread(grown[s], expand) * state + own
            if s < spans - 1:
                first[s, :, lanes(chunk)] = state
        total[:, lanes(chunk)] = state
        if chunk == 0:

            @pl.when(me < 2)
            def _():
                entered()

        @pl.when(me == 0)
        def _():
            for part in range(parts):
                hop = chunk * parts + part
                outbuf[hop] = state[:, part * HOP:(part + 1) * HOP].astype(BF16)
                if hop < EARLY:
                    onward(hop).start()

        if chunk == 0:
            loads[3].wait()

            def ask_near(q):
                @pl.when((q < me) | (q == me + 1))
                def _():
                    query(q, me).start()

            each(n, ask_near)
        if chunk == 3:
            for copy in loads[4 + len(cuts) - 1:]:
                copy.wait()

    def ask_far(q):
        @pl.when(q > me + 1)
        def _():
            pl.semaphore_wait(here.at[q], 1)
            query(q, me).start()

    each(n, ask_far)

    @pl.when(me == 0)
    def _():
        for hop in range(EARLY, hops):
            onward(hop).start()


    outer_parts = halves(jnp.exp(cum), 2)
    cum_t = cum.T
    row_kind = iota((8, heads), 0)
    row_value = jnp.where(
        row_kind == 0, jnp.exp(whole), jnp.where(row_kind == 1, skip_ref[...], jnp.exp(last[0]))
    )
    row_ref[...] = spread(halves(row_value, 3), expand_ref[...])

    scores = []
    for s in range(spans):
        at = slice(s * SPAN, (s + 1) * SPAN)
        scores.append([])
        for g in range(groups):
            cols = slice(g * N, (g + 1) * N)
            scores[s].append(dot_t(c_ref[at, cols], b_ref[at, cols]))
    causal = iota((SPAN, SPAN), 0) >= iota((SPAN, SPAN), 1)
    low = ones(iota((1, 2 * P_SIZE), 1) < P_SIZE)
    high = ones(iota((1, 2 * P_SIZE), 1) >= P_SIZE)

    def pair_input(start, s):
        x_pair = x_ref[s * SPAN:(s + 1) * SPAN, start:start + 2 * P_SIZE]
        return jnp.concatenate([x_pair * low, x_pair * high], axis=0)

    def weights(head, s):
        at = slice(s * SPAN, (s + 1) * SPAN)
        gap = jnp.where(causal, cum[at, head:head + 1] - cum_t[head:head + 1, at], FAR)
        main = scores[s][head // per_group] * jnp.exp(gap) * step_t[head:head + 1, at]
        return main.astype(BF16)

    def inner(hop):
        head, start = hop * HOP // P_SIZE, hop * HOP
        for s in range(spans):
            at = slice(s * SPAN, (s + 1) * SPAN)
            left = jnp.concatenate([weights(head, s), weights(head + 1, s)], axis=1)
            skipped = row_ref[1:2, start:start + HOP] * x_ref[at, start:start + HOP].astype(F32)
            base[at, start:start + HOP] = dot(left, pair_input(start, s)) + skipped

    def relay(hop):
        @pl.when(middle)
        def _():
            onward(hop).wait_recv()
            at = slice(hop * HOP, (hop + 1) * HOP)
            outbuf[hop] = (row_ref[0:1, at] * inbuf[hop].astype(F32) + total[:, at]).astype(BF16)
            onward(hop).start()

    def asked_by_others():
        def take(q):
            @pl.when(q != me)
            def _():
                query(me, q).wait_recv()

        each(n, take)
        for s in range(n):
            asked[s * STEPS:(s + 1) * STEPS, :] = queries[s, me].astype(F32)

        def lay(q):
            found = jnp.concatenate([queries[q, s].astype(F32) for s in range(n)], axis=0)
            asked_all[pl.ds(aligned(q * rows), rows), :] = found

        each(n, lay)

    for s in range(n):
        asked_own[s * STEPS:(s + 1) * STEPS, :] = queries[me, s].astype(F32)
        xd[s * STEPS:(s + 1) * STEPS, :] = dx_ref[s].astype(F32)
        bd[s * STEPS:(s + 1) * STEPS, :] = db_ref[s].astype(F32)
        dtd[s * STEPS:(s + 1) * STEPS, :] = ddt_ref[s].astype(F32)

    requests = len_ref.shape[1]
    final = len_ref[...] - 1
    row_r = iota((rows, requests), 0) // STEPS
    here_now = (final >= me * tokens) & (final < (me + 1) * tokens)
    chosen = here_now & (own_ref[...] == row_r)
    spot = jnp.sum(jnp.where(chosen, final - me * tokens, 0), axis=1, keepdims=True)
    place = iota((rows, tokens), 1)
    upto = (place <= spot) & (place // SPAN == spot // SPAN)
    cum_spot = picked(ones(place == spot), cum)
    spot_span = spot // SPAN
    spot_parts = halves(jnp.exp(cum_spot), 2)
    reach = cum_spot
    for s in range(spans - 1):
        reach = reach + jnp.where(spot_span > s, last[s], 0.0)
    reach_parts = halves(jnp.exp(reach), 2)
    for q in range(n):
        lgout[q] = jnp.where(row_kind == 0, reach[q * STEPS:q * STEPS + 1], whole)

    def tell(q):
        @pl.when(q < me)
        def _():
            log_to(q, me).start()

    each(n, tell)

    wanted = (
        (own_ref[...] == me) & (final >= row_r * tokens) & (final < (row_r + 1) * tokens)
    )
    present = jnp.sum(jnp.where(wanted, 1, 0), axis=1, keepdims=True) > 0
    r_row, r_col = iota((rows, rows), 0), iota((rows, rows), 1)
    slot = (r_row // STEPS) == (r_col // STEPS)
    row_h = iota((rows, heads), 0)

    def owner_start():
        dstep = softplus(dtd[...])
        running = picked(ones(slot & (r_col <= r_row)), rate * dstep)
        c_own = asked_own[...].astype(BF16)
        b_own = bd[...].astype(BF16)
        head_group = iota((rows, heads), 1) // per_group
        pairs = [
            dot_t(c_own[:, g * N:(g + 1) * N], b_own[:, g * N:(g + 1) * N]) for g in range(groups)
        ]
        fresh_parts, fresh_pick = [], []
        for k in range(STEPS):
            chosen_k = slot & (r_col % STEPS == k)
            pick = ones(chosen_k)
            score = jnp.zeros((rows, heads), F32)
            for g in range(groups):
                value = jnp.sum(jnp.where(chosen_k, pairs[g], 0.0), axis=1, keepdims=True)
                score = jnp.where(head_group == g, value, score)
            gap = jnp.where(row_h % STEPS >= k, running - picked(pick, running), FAR)
            fresh_parts.append(halves(jnp.exp(gap) * picked(pick, dstep) * score, 2))
            fresh_pick.append(pick)
        for chunk in range(chunks):
            expand = expand_ref[:, lanes(chunk)]
            xd_part = xd[:, lanes(chunk)]
            value = row_ref[1:2, lanes(chunk)] * xd_part
            for k in range(STEPS):
                value = value + spread(fresh_parts[k], expand) * dot(
                    fresh_pick[k], xd_part.astype(BF16)
                )
            res[:, lanes(chunk)] = value
        return running

    def owner_factors(running):
        def heard(q):
            @pl.when(q > me)
            def _():
                log_to(me, q).wait_recv()

        each(n, heard)
        row_s = row_h // STEPS
        exponent = reach
        for s in range(n):
            exponent = jnp.where((row_s == s) & (s > me), lgin[s, 0:1, :], exponent)
        for q in reversed(range(n)):
            level = jnp.where(row_s > q, exponent, jnp.where(row_s == q, 0.0, FAR))
            for k, piece in enumerate(halves(jnp.exp(running + level), 2)):
                factor[q, k] = piece
            through = jnp.where(q > me, lgin[q, 1:2, :], jnp.where(q == me, whole, 0.0))
            exponent = exponent + jnp.where(row_s > q, through, 0.0)
        level = jnp.where(row_s > me, exponent, jnp.where(row_s == me, reach, FAR))
        for k, piece in enumerate(halves(jnp.exp(running + level), 2)):
            factor[n, k] = piece
        for k, piece in enumerate(halves(jnp.exp(running), 2)):
            factor[n + 1, k] = piece

    def scale(index, chunk):
        expand = expand_ref[:, lanes(chunk)]
        return dot(factor[index, 0], expand) + dot(factor[index, 1], expand)

    def source_scores():
        found = asked[...].astype(BF16)
        return [
            [
                dot_t(found[:, g * N:(g + 1) * N], b_ref[s * SPAN:(s + 1) * SPAN, g * N:(g + 1) * N])
                for g in range(groups)
            ]
            for s in range(spans)
        ]

    def source_part(chunk, dec_scores):
        g = chunk * heads_chunk // per_group
        cols = slice(g * N, (g + 1) * N)
        found = asked[:, cols].astype(BF16)
        expand = expand_ref[:, lanes(chunk)]
        side = []
        for part in range(parts):
            hop = chunk * parts + part
            head, start = hop * HOP // P_SIZE, hop * HOP
            value = None
            for s in range(spans):
                at = slice(s * SPAN, (s + 1) * SPAN)
                left = []
                for h in (head, head + 1):
                    gap = jnp.where(upto[:, at], cum_spot[:, h:h + 1] - cum_t[h:h + 1, at], FAR)
                    left.append(
                        (dec_scores[s][g] * jnp.exp(gap) * step_t[h:h + 1, at]).astype(BF16)
                    )
                more = dot(jnp.concatenate(left, axis=1), pair_input(start, s))
                value = more if value is None else value + more
            side.append(value)
        value = jnp.concatenate(side, axis=1)
        held = jnp.zeros((rows, LANES), F32)
        for s in range(1, spans):
            begun = dot(found, first[s - 1, :, lanes(chunk)].astype(BF16))
            held = jnp.where(spot_span == s, begun, held)
        value = value + spread(spot_parts, expand) * held
        local[:, lanes(chunk)] = value
        state = total[:, lanes(chunk)].astype(BF16)
        if n <= 4:
            everything = dot(asked_all[:, cols].astype(BF16), state)

        def lay(i):
            local_i = local[pl.ds(aligned(i * 2 * STEPS), 2 * STEPS), lanes(chunk)]
            for half in range(2):
                q = 2 * i + half
                if n <= 4:
                    found_q = everything[q * rows:(q + 1) * rows]
                else:
                    left = asked_all[pl.ds(aligned(q * rows), rows), cols]
                    found_q = dot(left.astype(BF16), state)
                for s in range(n):
                    zbuf[q, s, :, lanes(chunk)] = jnp.where(
                        me == s,
                        local_i[half * STEPS:(half + 1) * STEPS],
                        found_q[s * STEPS:(s + 1) * STEPS],
                    ).astype(BF16)

        each(n // 2, lay)

    def add_z(ref, q, chunk):
        value = jnp.concatenate([ref[q, s, :, lanes(chunk)].astype(F32) for s in range(n)], axis=0)
        kept = iota((rows, 1), 0) // STEPS >= q
        res[:, lanes(chunk)] += jnp.where(kept, scale(q, chunk) * value, 0.0)

    def arrived(chunk):
        return jnp.concatenate([inbuf[chunk * parts + p] for p in range(parts)], axis=1)

    def carry(chunk, alone=False):
        g = chunk * heads_chunk // per_group
        cols = slice(g * N, (g + 1) * N)
        expand = expand_ref[:, lanes(chunk)]
        outer = spread(outer_parts, expand)
        if not alone:
            incoming = arrived(chunk)
        for s in range(spans):
            at = slice(s * SPAN, (s + 1) * SPAN)
            if alone and s == 0:
                out_ref[at, lanes(chunk)] = base[at, lanes(chunk)].astype(BF16)
                continue
            if s == 0:
                held = incoming
                passed = None
            elif alone:
                held = first[s - 1, :, lanes(chunk)].astype(BF16)
            else:
                step_on = row_ref[2:3, lanes(chunk)] if s == 1 else spread(grown[s - 1], expand)
                passed = step_on if passed is None else passed * step_on
                held = (
                    passed * incoming.astype(F32) + first[s - 1, :, lanes(chunk)]
                ).astype(BF16)
            out_ref[at, lanes(chunk)] = (
                base[at, lanes(chunk)] + outer[at] * dot(c_ref[at, cols], held)
            ).astype(BF16)

    def carry_requests(chunk):
        g = chunk * heads_chunk // per_group
        cols = slice(g * N, (g + 1) * N)
        left = jnp.concatenate([asked[:, cols], asked_own[:, cols]], axis=0).astype(BF16)
        carried = dot(left, arrived(chunk))
        reached[:, lanes(chunk)] = (
            spread(reach_parts, expand_ref[:, lanes(chunk)]) * carried[:rows]
        )
        res[:, lanes(chunk)] += scale(n, chunk) * carried[rows:]

    def give(piece):
        wide = width // PIECES
        area = slice(piece * wide, (piece + 1) * wide)
        value = (reached[:, area] + local[:, area]).astype(BF16)
        for q in range(n):
            rbuf[piece, q] = value[q * STEPS:(q + 1) * STEPS]

        def hand(q):
            @pl.when(q > me)
            def _():
                r_to(q, me, piece).start()

        each(n, hand)

    running = None
    dec_scores = None
    for chunk in range(chunks):
        for part in range(parts):
            inner(chunk * parts + part)
            relay(chunk * parts + part)
        if chunk == chunks - 1:

            @pl.when(middle)
            def _():
                carry_requests(chunk)
                give(1)

        @pl.when(middle)
        def _():
            carry(chunk)

        if chunk == 0:
            running = owner_start()
        if chunk == 1:
            asked_by_others()
            dec_scores = source_scores()
        if 2 <= chunk < 4:
            for more in range((chunk - 2) * chunks // 2, (chunk - 1) * chunks // 2):
                source_part(more, dec_scores)
        if chunk == 3:

            def answer(q):
                @pl.when(q < me)
                def _():
                    slots_from(me, lambda s: z_to(q, me, s).start())

            each(n, answer)
        if chunk == 4:
            owner_factors(running)

            @pl.when(middle)
            def _():
                for more in range(chunks // PIECES):
                    carry_requests(more)
                give(0)

        if chunk == 5:
            for more in range(chunks):
                add_z(zbuf, me, more)
        if chunk == 6:

            @pl.when(middle)
            def _():
                for more in range(chunks // PIECES, chunks - 1):
                    carry_requests(more)

    @pl.when(me == n - 1)
    def _():
        for chunk in range(chunks):
            for part in range(parts):
                onward(chunk * parts + part).wait_recv()
            carry(chunk)
            carry_requests(chunk)

    @pl.when(me == 0)
    def _():
        for chunk in range(chunks):
            carry(chunk, alone=True)
        reached[...] = jnp.zeros(reached.shape, F32)
        for piece in range(PIECES):
            give(piece)

    def collect(q):
        @pl.when(q > me)
        def _():
            slots_from(q, lambda s: z_to(me, q, s).wait_recv())
            for chunk in range(chunks):
                add_z(zin, q, chunk)

    each(n, collect)

    def receive(q):
        @pl.when(q < me)
        def _():
            for piece in range(PIECES):
                r_to(me, q, piece).wait_recv()
            wide = width // PIECES
            for chunk in range(chunks):
                at = chunk * LANES % wide
                value = rin[chunk * LANES // wide, q, :, at:at + LANES].astype(F32)
                grow = dot(running_rows[0], expand_ref[:, lanes(chunk)]) + dot(
                    running_rows[1], expand_ref[:, lanes(chunk)]
                )
                kept = jnp.where(iota((rows, 1), 0) // STEPS == q, grow, 0.0)
                tall = jnp.concatenate([value] * n, axis=0)
                res[:, lanes(chunk)] += kept * tall

    running_rows = [factor[n + 1, 0], factor[n + 1, 1]]
    each(n, receive)
    done = jnp.where(present, res[...], 0.0).astype(BF16)
    for s in range(n):
        dout_ref[0, s] = done[s * STEPS:(s + 1) * STEPS]

    @pl.when(me < n - 1)
    def _():
        for hop in range(hops):
            onward(hop).wait_send()

    def finish(q):
        @pl.when(q != me)
        def _():
            query(q, me).wait_send()

        @pl.when(q < me)
        def _():
            log_to(q, me).wait_send()
            slots_from(me, lambda s: z_to(q, me, s).wait_send())

        @pl.when(q > me)
        def _():
            for piece in range(PIECES):
                r_to(q, me, piece).wait_send()

    each(n, finish)


def store(out_vmem, dout_vmem, out_hbm, dout_hbm, sem):
    copies = [
        pltpu.make_async_copy(out_vmem, out_hbm, sem.at[0]),
        pltpu.make_async_copy(dout_vmem, dout_hbm, sem.at[1]),
    ]
    for copy in copies:
        copy.start()
    for copy in copies:
        copy.wait()


def shards(
    ssm_input, bmat, cmat, dt_raw, a_log, d_skip, prompt_len, owner, dec_x, dec_b, dec_c, dec_dt
):
    n = lax.axis_size("seq")
    tokens, width = ssm_input.shape
    heads = dt_raw.shape[1]
    gn = bmat.shape[1]
    spans = tokens // SPAN
    hops = width // HOP
    rows = n * STEPS
    requests = prompt_len.shape[0]
    hbm = pl.BlockSpec(memory_space=pltpu.HBM)
    vmem = pl.BlockSpec(memory_space=pltpu.VMEM)
    dma = pltpu.SemaphoreType.DMA
    slots = (n, STEPS)
    operands = (
        ssm_input, bmat, cmat, dt_raw.T, a_log[None, :], d_skip[None, :],
        prompt_len[None, :], owner[None, :], dec_x, dec_b, dec_c, dec_dt,
    )
    out, dout = pl.pallas_call(
        functools.partial(kernel, n),
        out_shape=(
            pltpu.VMEM((tokens, width), BF16),
            pltpu.VMEM((1,) + slots + (width,), BF16),
        ),
        in_specs=[hbm] * 12,
        out_specs=(vmem, vmem),
        scratch_shapes=[
            pltpu.VMEM((tokens, width), BF16),
            pltpu.VMEM((tokens, gn), BF16),
            pltpu.VMEM((tokens, gn), BF16),
            pltpu.VMEM((heads, tokens), BF16),
            pltpu.VMEM((1, heads), F32),
            pltpu.VMEM((1, heads), F32),
            pltpu.VMEM((1, requests), jnp.int32),
            pltpu.VMEM((1, requests), jnp.int32),
            pltpu.VMEM(slots + (width,), BF16),
            pltpu.VMEM(slots + (gn,), BF16),
            pltpu.VMEM(slots + (heads,), BF16),
            pltpu.VMEM((n,) + slots + (gn,), BF16),
            pltpu.VMEM((rows, width), F32),
            pltpu.VMEM((rows, gn), F32),
            pltpu.VMEM((rows, heads), F32),
            pltpu.VMEM((rows, gn), F32),
            pltpu.VMEM((rows, gn), F32),
            pltpu.VMEM((n * rows, gn), F32),
            pltpu.VMEM((heads, width), BF16),
            pltpu.VMEM((8, width), F32),
            pltpu.VMEM((max(spans - 1, 1), N, width), F32),
            pltpu.VMEM((N, width), F32),
            pltpu.VMEM((tokens, width), F32),
            pltpu.VMEM((hops, N, HOP), BF16),
            pltpu.VMEM((hops, N, HOP), BF16),
            pltpu.VMEM((rows, width), F32),
            pltpu.VMEM((rows, width), F32),
            pltpu.VMEM((rows, width), F32),
            pltpu.VMEM((n,) + slots + (width,), BF16),
            pltpu.VMEM((n,) + slots + (width,), BF16),
            pltpu.VMEM((PIECES, n, STEPS, width // PIECES), BF16),
            pltpu.VMEM((PIECES, n, STEPS, width // PIECES), BF16),
            pltpu.VMEM((n, 8, heads), F32),
            pltpu.VMEM((n, 8, heads), F32),
            pltpu.VMEM((n + 2, 2, rows, heads), BF16),
            dma((15,)),
            dma((hops,)),
            dma((hops,)),
            dma((n,)),
            dma((n,)),
            dma((n,)),
            dma((n,)),
            dma((n, n)),
            dma((n, n)),
            dma((PIECES, n)),
            dma((PIECES, n)),
            pltpu.SemaphoreType.REGULAR((n,)),
        ],
        compiler_params=pltpu.CompilerParams(
            collective_id=0, has_side_effects=True, vmem_limit_bytes=56 * 1024 * 1024
        ),
    )(*(pltpu.with_memory_space_constraint(operand, pltpu.HBM) for operand in operands))
    return pl.pallas_call(
        store,
        out_shape=(
            jax.ShapeDtypeStruct(out.shape, BF16),
            jax.ShapeDtypeStruct(dout.shape, BF16),
        ),
        in_specs=[vmem, vmem],
        out_specs=(hbm, hbm),
        scratch_shapes=[dma((2,))],
    )(
        pltpu.with_memory_space_constraint(out, pltpu.VMEM),
        pltpu.with_memory_space_constraint(dout, pltpu.VMEM),
    )


def solution(mesh):
    placed = (
        P(("grp", "seq"), "tp"),
        P(("grp", "seq"), "tp"),
        P(("grp", "seq"), "tp"),
        P(("grp", "seq"), "tp"),
        P("tp"),
        P("tp"),
        P("grp"),
        P("grp"),
        P(("grp", "seq"), None, None, "tp"),
        P(("grp", "seq"), None, None, "tp"),
        P(("grp", "seq"), None, None, "tp"),
        P(("grp", "seq"), None, None, "tp"),
    )
    return jax.shard_map(
        shards,
        mesh=mesh,
        in_specs=placed,
        out_specs=(P(("grp", "seq"), "tp"), P(("grp", "seq"), None, None, "tp")),
        check_vma=False,
    )
```

```python
import functools

import jax
import jax.numpy as jnp
from jax import lax
from jax.experimental import pallas as pl
from jax.experimental.pallas import tpu as pltpu
from jax.sharding import PartitionSpec as P

P_SIZE = 64
N = 128
SPAN = 128
STEPS = 4
LANES = 256
HOP = 128
PIECES = 2
EARLY = 6
AHEAD = 4
MESH = pl.DeviceIdType.MESH
F32 = jnp.float32
BF16 = jnp.bfloat16
FAR = -1e30


def iota(shape, axis):
    return lax.broadcasted_iota(jnp.int32, shape, axis)


def dot(a, b):
    return jnp.dot(a, b, preferred_element_type=F32)


def dot_t(a, b):
    return lax.dot_general(a, b, (((1,), (1,)), ((), ())), preferred_element_type=F32)


def halves(value, count):
    pieces = []
    for _ in range(count):
        piece = value.astype(BF16)
        pieces.append(piece)
        value = value - piece.astype(F32)
    return pieces


def picked(selector, value, count=3):
    parts = [dot(selector, piece) for piece in halves(value, count)]
    return sum(parts[1:], parts[0])


def spread(pieces, expand):
    parts = [dot(piece, expand) for piece in pieces]
    return sum(parts[1:], parts[0])


def ones(mask):
    return jnp.where(mask, 1.0, 0.0).astype(BF16)


def softplus(value):
    return jnp.maximum(value, 0.0) + jnp.log1p(jnp.exp(-jnp.abs(value)))


def aligned(index):
    return index if isinstance(index, int) else pl.multiple_of(index, 8)


def each(count, body):
    if count <= 4:
        for i in range(count):
            body(i)
    else:

        def turn(i, carry):
            body(i)
            return carry

        lax.fori_loop(0, count, turn, 0)


def kernel(
    n,
    x_hbm, b_hbm, c_hbm, dt_hbm, alog_hbm, skip_hbm, len_hbm, own_hbm,
    dx_hbm, db_hbm, dc_hbm, ddt_hbm,
    out_ref, dout_ref,
    x_ref, b_ref, c_ref, dt_ref, alog_ref, skip_ref, len_ref, own_ref,
    dx_ref, db_ref, ddt_ref, queries,
    xd, bd, dtd, asked, asked_own, asked_all,
    expand_ref, row_ref, first, total, base, inbuf, outbuf,
    res, local, reached, zbuf, zin, rbuf, rin, lgout, lgin, factor,
    load_sem, send_state, recv_state, send_query, recv_query,
    send_log, recv_log, send_z, recv_z, send_r, recv_r, here,
):
    me = lax.axis_index("seq")
    tokens, width = x_ref.shape
    heads = dt_ref.shape[0]
    groups = b_ref.shape[1] // N
    per_group = heads // groups
    spans = tokens // SPAN
    chunks = width // LANES
    heads_chunk = LANES // P_SIZE
    hops = width // HOP
    parts = LANES // HOP
    rows = n * STEPS
    middle = (me > 0) & (me < n - 1)
    ending = (me == 0) | (me == n - 1)

    def lanes(chunk):
        return slice(chunk * LANES, (chunk + 1) * LANES)

    barrier = pltpu.get_barrier_semaphore()

    def greet(q):
        @pl.when((q > me) | (q == me - 1))
        def _():
            pl.semaphore_signal(barrier, inc=1, device_id={"seq": q}, device_id_type=MESH)

    sources = [
        (dt_hbm, dt_ref),
        (alog_hbm, alog_ref),
        (b_hbm, b_ref),
        (dc_hbm.at[0], queries.at[me]),
    ]
    cuts = [0, LANES, 2 * LANES, 4 * LANES, width]
    for begin, end in zip(cuts[:-1], cuts[1:]):
        sources.append((x_hbm.at[:, begin:end], x_ref.at[:, begin:end]))
    sources += [
        (c_hbm, c_ref),
        (skip_hbm, skip_ref),
        (len_hbm, len_ref),
        (own_hbm, own_ref),
        (ddt_hbm.at[0], ddt_ref),
        (db_hbm.at[0], db_ref),
        (dx_hbm.at[0], dx_ref),
    ]
    loads = [
        pltpu.make_async_copy(source, landing, load_sem.at[k])
        for k, (source, landing) in enumerate(sources)
    ]
    for copy in loads[:5]:
        copy.start()
    each(n, greet)

    def push(source, landing, sends, recvs, target):
        return pltpu.make_async_remote_copy(
            src_ref=source, dst_ref=landing, send_sem=sends, recv_sem=recvs,
            device_id={"seq": target}, device_id_type=MESH,
        )

    def query(q, origin):
        return push(
            queries.at[origin], queries.at[origin], send_query.at[q], recv_query.at[origin], q
        )

    def log_to(q, origin):
        return push(lgout.at[q], lgin.at[origin], send_log.at[q], recv_log.at[origin], q)

    def z_to(q, origin, s):
        return push(
            zbuf.at[q, s], zin.at[origin, s], send_z.at[q, s], recv_z.at[origin, s], q
        )

    def slots_from(origin, body):
        def turn(s):
            @pl.when(s >= origin)
            def _():
                body(s)

        each(n, turn)

    def r_to(q, origin, piece):
        return push(
            rbuf.at[piece, q], rin.at[piece, origin],
            send_r.at[piece, q], recv_r.at[piece, origin], q,
        )

    def onward(hop):
        return push(
            outbuf.at[hop], inbuf.at[hop], send_state.at[hop], recv_state.at[hop],
            lax.rem(me + 1, n),
        )

    def entered():
        pl.semaphore_wait(barrier, me + jnp.where(me < n - 1, 1, 0))

    @pl.when(me >= 2)
    def _():
        entered()

        def announce(q):
            @pl.when(q < me - 1)
            def _():
                pl.semaphore_signal(here.at[me], inc=1, device_id={"seq": q}, device_id_type=MESH)

        each(n, announce)

    expand_ref[...] = ones(iota((heads, width), 0) == iota((heads, width), 1) // P_SIZE)
    t_row, t_col = iota((tokens, tokens), 0), iota((tokens, tokens), 1)
    upper = ones(((t_row // SPAN) == (t_col // SPAN)) & (t_col <= t_row))
    loads[0].wait()
    loads[1].wait()
    for copy in loads[5:]:
        copy.start()
    step_t = softplus(dt_ref[...].astype(F32))
    step = step_t.T
    rate = -jnp.exp(alog_ref[...])
    cum = picked(upper, rate * step)
    last = [cum[(s + 1) * SPAN - 1:(s + 1) * SPAN, :] for s in range(spans)]
    whole = sum(last[1:], last[0])
    into = jnp.concatenate(
        [
            jnp.exp(last[s] - cum[s * SPAN:(s + 1) * SPAN]) * step[s * SPAN:(s + 1) * SPAN]
            for s in range(spans)
        ],
        axis=0,
    )
    into_parts = halves(into, 2)
    grown = [halves(jnp.exp(last[s]), 2) for s in range(spans)]
    loads[2].wait()
    b_t = [
        [b_ref[s * SPAN:(s + 1) * SPAN, g * N:(g + 1) * N].T for g in range(groups)]
        for s in range(spans)
    ]

    def relay(hop, who):
        @pl.when(who)
        def _():
            onward(hop).wait_recv()
            at = slice(hop * HOP, (hop + 1) * HOP)
            outbuf[hop] = (row_ref[0:1, at] * inbuf[hop].astype(F32) + total[:, at]).astype(BF16)
            onward(hop).start()

    second = (me == 1) & (me < n - 1)
    later = (me > 1) & (me < n - 1)
    for chunk in range(chunks):
        if chunk * LANES in cuts:
            loads[4 + cuts.index(chunk * LANES)].wait()
        g = chunk * heads_chunk // per_group
        expand = expand_ref[:, lanes(chunk)]
        weighted = (x_ref[:, lanes(chunk)].astype(F32) * spread(into_parts, expand)).astype(BF16)
        state = None
        for s in range(spans):
            own = dot(b_t[s][g], weighted[s * SPAN:(s + 1) * SPAN])
            state = own if state is None else spread(grown[s], expand) * state + own
            if s < spans - 1:
                first[s, :, lanes(chunk)] = state
        total[:, lanes(chunk)] = state
        if chunk == 0:

            @pl.when(me < 2)
            def _():
                entered()

        @pl.when(me == 0)
        def _():
            for part in range(parts):
                hop = chunk * parts + part
                outbuf[hop] = state[:, part * HOP:(part + 1) * HOP].astype(BF16)
                if hop < EARLY:
                    onward(hop).start()

        if chunk == 0:
            loads[3].wait()

            def ask_near(q):
                @pl.when((q < me) | (q == me + 1))
                def _():
                    query(q, me).start()

            each(n, ask_near)
        if chunk == 3:
            for copy in loads[4 + len(cuts) - 1:]:
                copy.wait()
            row_kind = iota((8, heads), 0)
            row_value = jnp.where(
                row_kind == 0, jnp.exp(whole), jnp.where(row_kind == 1, skip_ref[...], jnp.exp(last[0]))
            )
            row_ref[...] = spread(halves(row_value, 3), expand_ref[...])
        if chunk >= chunks - AHEAD:
            relay(chunk - chunks + AHEAD, second)

    def ask_far(q):
        @pl.when(q > me + 1)
        def _():
            pl.semaphore_wait(here.at[q], 1)
            query(q, me).start()

    each(n, ask_far)

    @pl.when(me == 0)
    def _():
        for hop in range(EARLY, hops):
            onward(hop).start()


    outer_parts = halves(jnp.exp(cum), 2)
    cum_t = cum.T
    scores = []
    for s in range(spans):
        at = slice(s * SPAN, (s + 1) * SPAN)
        scores.append([])
        for g in range(groups):
            cols = slice(g * N, (g + 1) * N)
            scores[s].append(dot_t(c_ref[at, cols], b_ref[at, cols]))
    causal = iota((SPAN, SPAN), 0) >= iota((SPAN, SPAN), 1)
    low = ones(iota((1, 2 * P_SIZE), 1) < P_SIZE)
    high = ones(iota((1, 2 * P_SIZE), 1) >= P_SIZE)

    def pair_input(start, s):
        x_pair = x_ref[s * SPAN:(s + 1) * SPAN, start:start + 2 * P_SIZE]
        return jnp.concatenate([x_pair * low, x_pair * high], axis=0)

    def weights(head, s):
        at = slice(s * SPAN, (s + 1) * SPAN)
        gap = jnp.where(causal, cum[at, head:head + 1] - cum_t[head:head + 1, at], FAR)
        main = scores[s][head // per_group] * jnp.exp(gap) * step_t[head:head + 1, at]
        return main.astype(BF16)

    def inner(hop):
        head, start = hop * HOP // P_SIZE, hop * HOP
        for s in range(spans):
            at = slice(s * SPAN, (s + 1) * SPAN)
            left = jnp.concatenate([weights(head, s), weights(head + 1, s)], axis=1)
            skipped = row_ref[1:2, start:start + HOP] * x_ref[at, start:start + HOP].astype(F32)
            base[at, start:start + HOP] = dot(left, pair_input(start, s)) + skipped

    def asked_by_others():
        def take(q):
            @pl.when(q != me)
            def _():
                query(me, q).wait_recv()

        each(n, take)
        for s in range(n):
            asked[s * STEPS:(s + 1) * STEPS, :] = queries[s, me].astype(F32)

        def lay(q):
            found = jnp.concatenate([queries[q, s].astype(F32) for s in range(n)], axis=0)
            asked_all[pl.ds(aligned(q * rows), rows), :] = found

        each(n, lay)

    for s in range(n):
        asked_own[s * STEPS:(s + 1) * STEPS, :] = queries[me, s].astype(F32)
        xd[s * STEPS:(s + 1) * STEPS, :] = dx_ref[s].astype(F32)
        bd[s * STEPS:(s + 1) * STEPS, :] = db_ref[s].astype(F32)
        dtd[s * STEPS:(s + 1) * STEPS, :] = ddt_ref[s].astype(F32)

    requests = len_ref.shape[1]
    final = len_ref[...] - 1
    row_r = iota((rows, requests), 0) // STEPS
    here_now = (final >= me * tokens) & (final < (me + 1) * tokens)
    chosen = here_now & (own_ref[...] == row_r)
    spot = jnp.sum(jnp.where(chosen, final - me * tokens, 0), axis=1, keepdims=True)
    place = iota((rows, tokens), 1)
    upto = (place <= spot) & (place // SPAN == spot // SPAN)
    cum_spot = picked(ones(place == spot), cum)
    spot_span = spot // SPAN
    spot_parts = halves(jnp.exp(cum_spot), 2)
    reach = cum_spot
    for s in range(spans - 1):
        reach = reach + jnp.where(spot_span > s, last[s], 0.0)
    reach_parts = halves(jnp.exp(reach), 2)
    for q in range(n):
        lgout[q] = jnp.where(row_kind == 0, reach[q * STEPS:q * STEPS + 1], whole)

    def tell(q):
        @pl.when(q < me)
        def _():
            log_to(q, me).start()

    each(n, tell)

    wanted = (
        (own_ref[...] == me) & (final >= row_r * tokens) & (final < (row_r + 1) * tokens)
    )
    present = jnp.sum(jnp.where(wanted, 1, 0), axis=1, keepdims=True) > 0
    r_row, r_col = iota((rows, rows), 0), iota((rows, rows), 1)
    slot = (r_row // STEPS) == (r_col // STEPS)
    row_h = iota((rows, heads), 0)

    def owner_start():
        dstep = softplus(dtd[...])
        running = picked(ones(slot & (r_col <= r_row)), rate * dstep)
        c_own = asked_own[...].astype(BF16)
        b_own = bd[...].astype(BF16)
        head_group = iota((rows, heads), 1) // per_group
        pairs = [
            dot_t(c_own[:, g * N:(g + 1) * N], b_own[:, g * N:(g + 1) * N]) for g in range(groups)
        ]
        fresh_parts, fresh_pick = [], []
        for k in range(STEPS):
            chosen_k = slot & (r_col % STEPS == k)
            pick = ones(chosen_k)
            score = jnp.zeros((rows, heads), F32)
            for g in range(groups):
                value = jnp.sum(jnp.where(chosen_k, pairs[g], 0.0), axis=1, keepdims=True)
                score = jnp.where(head_group == g, value, score)
            gap = jnp.where(row_h % STEPS >= k, running - picked(pick, running), FAR)
            fresh_parts.append(halves(jnp.exp(gap) * picked(pick, dstep) * score, 2))
            fresh_pick.append(pick)
        return running, fresh_parts, fresh_pick

    def owner_part(chunk, fresh_parts, fresh_pick):
        expand = expand_ref[:, lanes(chunk)]
        xd_part = xd[:, lanes(chunk)]
        value = row_ref[1:2, lanes(chunk)] * xd_part
        for k in range(STEPS):
            value = value + spread(fresh_parts[k], expand) * dot(
                fresh_pick[k], xd_part.astype(BF16)
            )
        res[:, lanes(chunk)] = value

    def owner_factors(running):
        def heard(q):
            @pl.when(q > me)
            def _():
                log_to(me, q).wait_recv()

        each(n, heard)
        row_s = row_h // STEPS
        exponent = reach
        for s in range(n):
            exponent = jnp.where((row_s == s) & (s > me), lgin[s, 0:1, :], exponent)
        for q in reversed(range(n)):
            level = jnp.where(row_s > q, exponent, jnp.where(row_s == q, 0.0, FAR))
            for k, piece in enumerate(halves(jnp.exp(running + level), 2)):
                factor[q, k] = piece
            through = jnp.where(q > me, lgin[q, 1:2, :], jnp.where(q == me, whole, 0.0))
            exponent = exponent + jnp.where(row_s > q, through, 0.0)
        level = jnp.where(row_s > me, exponent, jnp.where(row_s == me, reach, FAR))
        for k, piece in enumerate(halves(jnp.exp(running + level), 2)):
            factor[n, k] = piece
        for k, piece in enumerate(halves(jnp.exp(running), 2)):
            factor[n + 1, k] = piece

    def scale(index, chunk):
        expand = expand_ref[:, lanes(chunk)]
        return dot(factor[index, 0], expand) + dot(factor[index, 1], expand)

    def source_scores():
        found = asked[...].astype(BF16)
        return [
            [
                dot_t(found[:, g * N:(g + 1) * N], b_ref[s * SPAN:(s + 1) * SPAN, g * N:(g + 1) * N])
                for g in range(groups)
            ]
            for s in range(spans)
        ]

    def source_part(chunk, dec_scores):
        g = chunk * heads_chunk // per_group
        cols = slice(g * N, (g + 1) * N)
        found = asked[:, cols].astype(BF16)
        expand = expand_ref[:, lanes(chunk)]
        side = []
        for part in range(parts):
            hop = chunk * parts + part
            head, start = hop * HOP // P_SIZE, hop * HOP
            value = None
            for s in range(spans):
                at = slice(s * SPAN, (s + 1) * SPAN)
                left = []
                for h in (head, head + 1):
                    gap = jnp.where(upto[:, at], cum_spot[:, h:h + 1] - cum_t[h:h + 1, at], FAR)
                    left.append(
                        (dec_scores[s][g] * jnp.exp(gap) * step_t[h:h + 1, at]).astype(BF16)
                    )
                more = dot(jnp.concatenate(left, axis=1), pair_input(start, s))
                value = more if value is None else value + more
            side.append(value)
        value = jnp.concatenate(side, axis=1)
        held = jnp.zeros((rows, LANES), F32)
        for s in range(1, spans):
            begun = dot(found, first[s - 1, :, lanes(chunk)].astype(BF16))
            held = jnp.where(spot_span == s, begun, held)
        value = value + spread(spot_parts, expand) * held
        local[:, lanes(chunk)] = value
        state = total[:, lanes(chunk)].astype(BF16)
        if n <= 4:
            everything = dot(asked_all[:, cols].astype(BF16), state)

        def lay(i):
            local_i = local[pl.ds(aligned(i * 2 * STEPS), 2 * STEPS), lanes(chunk)]
            for half in range(2):
                q = 2 * i + half
                if n <= 4:
                    found_q = everything[q * rows:(q + 1) * rows]
                else:
                    left = asked_all[pl.ds(aligned(q * rows), rows), cols]
                    found_q = dot(left.astype(BF16), state)
                for s in range(n):
                    zbuf[q, s, :, lanes(chunk)] = jnp.where(
                        me == s,
                        local_i[half * STEPS:(half + 1) * STEPS],
                        found_q[s * STEPS:(s + 1) * STEPS],
                    ).astype(BF16)

        each(n // 2, lay)

    def add_z(ref, q, chunk):
        value = jnp.concatenate([ref[q, s, :, lanes(chunk)].astype(F32) for s in range(n)], axis=0)
        kept = iota((rows, 1), 0) // STEPS >= q
        res[:, lanes(chunk)] += jnp.where(kept, scale(q, chunk) * value, 0.0)

    def arrived(begin, end):
        return jnp.concatenate([inbuf[h] for h in range(begin // HOP, end // HOP)], axis=1)

    def carry(begin, end, alone=False):
        g = begin // P_SIZE // per_group
        cols = slice(g * N, (g + 1) * N)
        area = slice(begin, end)
        expand = expand_ref[:, area]
        outer = spread(outer_parts, expand)
        if not alone:
            incoming = arrived(begin, end)
        for s in range(spans):
            at = slice(s * SPAN, (s + 1) * SPAN)
            if alone and s == 0:
                out_ref[at, area] = base[at, area].astype(BF16)
                continue
            if s == 0:
                held = incoming
                passed = None
            elif alone:
                held = first[s - 1, :, area].astype(BF16)
            else:
                step_on = row_ref[2:3, area] if s == 1 else spread(grown[s - 1], expand)
                passed = step_on if passed is None else passed * step_on
                held = (passed * incoming.astype(F32) + first[s - 1, :, area]).astype(BF16)
            out_ref[at, area] = (
                base[at, area] + outer[at] * dot(c_ref[at, cols], held)
            ).astype(BF16)

    def carry_requests(chunk):
        g = chunk * heads_chunk // per_group
        cols = slice(g * N, (g + 1) * N)
        left = jnp.concatenate([asked[:, cols], asked_own[:, cols]], axis=0).astype(BF16)
        carried = dot(left, arrived(chunk * LANES, (chunk + 1) * LANES))
        reached[:, lanes(chunk)] = (
            spread(reach_parts, expand_ref[:, lanes(chunk)]) * carried[:rows]
        )
        res[:, lanes(chunk)] += scale(n, chunk) * carried[rows:]

    def give(piece):
        wide = width // PIECES
        area = slice(piece * wide, (piece + 1) * wide)
        value = (reached[:, area] + local[:, area]).astype(BF16)
        for q in range(n):
            rbuf[piece, q] = value[q * STEPS:(q + 1) * STEPS]

        def hand(q):
            @pl.when(q > me)
            def _():
                r_to(q, me, piece).start()

        each(n, hand)

    def receive(piece):
        def take(q):
            @pl.when(q < me)
            def _():
                r_to(me, q, piece).wait_recv()

        each(n, take)
        wide = width // PIECES
        kept = iota((rows, 1), 0) // STEPS < me
        for chunk in range(piece * chunks // PIECES, (piece + 1) * chunks // PIECES):
            at = chunk * LANES % wide
            value = jnp.concatenate(
                [rin[piece, q, :, at:at + LANES].astype(F32) for q in range(n)], axis=0
            )
            res[:, lanes(chunk)] += jnp.where(kept, scale(n + 1, chunk) * value, 0.0)

    def answer(q):
        @pl.when(q < me)
        def _():
            slots_from(me, lambda s: z_to(q, me, s).start())

    half = hops // 2
    kept = {}
    for hop in range(hops):
        inner(hop)
        if hop + AHEAD < hops:
            relay(hop + AHEAD, second)
        relay(hop, later)
        chunk = hop // parts
        if hop % parts == parts - 1:
            if chunk == chunks - 1:

                @pl.when(later)
                def _():
                    carry_requests(chunk)
                    give(1)

            @pl.when(middle)
            def _():
                carry(chunk * LANES, (chunk + 1) * LANES)

        if hop == 0:
            kept["running"], kept["parts"], kept["pick"] = owner_start()
        if hop == 3:
            asked_by_others()
            kept["scores"] = source_scores()
        if 4 <= hop < 8:
            for more in range((hop - 4) * chunks // 4, (hop - 3) * chunks // 4):
                source_part(more, kept["scores"])
        if hop == 7:
            each(n, answer)
        if hop == 8:
            owner_factors(kept["running"])
        if 9 <= hop < 13:
            for more in range((hop - 9) * chunks // 4, (hop - 8) * chunks // 4):
                owner_part(more, kept["parts"], kept["pick"])
                add_z(zbuf, me, more)
        if hop == 13:

            @pl.when(middle)
            def _():
                for more in range(chunks // PIECES):
                    carry_requests(more)
                give(0)

        if hop == 14:

            @pl.when(middle)
            def _():
                for more in range(chunks // PIECES, chunks - 1):
                    carry_requests(more)

    @pl.when(second)
    def _():
        carry_requests(chunks - 1)
        give(1)

    @pl.when(me == n - 1)
    def _():
        for chunk in range(chunks):
            for part in range(parts):
                hop = chunk * parts + part
                onward(hop).wait_recv()
                if chunk == chunks - 1:
                    carry(hop * HOP, (hop + 1) * HOP)
            if chunk < chunks - 1:
                carry(chunk * LANES, (chunk + 1) * LANES)
            carry_requests(chunk)
            if chunk == chunks - 2:
                receive(0)
        receive(1)

    @pl.when(me == 0)
    def _():
        reached[...] = jnp.zeros(reached.shape, F32)
        for piece in range(PIECES):
            give(piece)
        for chunk in range(chunks):
            carry(chunk * LANES, (chunk + 1) * LANES, alone=True)

    def collect(q):
        @pl.when(q > me)
        def _():
            slots_from(q, lambda s: z_to(me, q, s).wait_recv())
            for chunk in range(chunks):
                add_z(zin, q, chunk)

    each(n, collect)

    @pl.when(middle)
    def _():
        for piece in range(PIECES):
            receive(piece)

    done = jnp.where(present, res[...], 0.0).astype(BF16)
    for s in range(n):
        dout_ref[0, s] = done[s * STEPS:(s + 1) * STEPS]

    @pl.when(me < n - 1)
    def _():
        for hop in range(hops):
            onward(hop).wait_send()

    def finish(q):
        @pl.when(q != me)
        def _():
            query(q, me).wait_send()

        @pl.when(q < me)
        def _():
            log_to(q, me).wait_send()
            slots_from(me, lambda s: z_to(q, me, s).wait_send())

        @pl.when(q > me)
        def _():
            for piece in range(PIECES):
                r_to(q, me, piece).wait_send()

    each(n, finish)


def store(out_vmem, dout_vmem, out_hbm, dout_hbm, sem):
    copies = [
        pltpu.make_async_copy(out_vmem, out_hbm, sem.at[0]),
        pltpu.make_async_copy(dout_vmem, dout_hbm, sem.at[1]),
    ]
    for copy in copies:
        copy.start()
    for copy in copies:
        copy.wait()


def shards(
    ssm_input, bmat, cmat, dt_raw, a_log, d_skip, prompt_len, owner, dec_x, dec_b, dec_c, dec_dt
):
    n = lax.axis_size("seq")
    tokens, width = ssm_input.shape
    heads = dt_raw.shape[1]
    gn = bmat.shape[1]
    spans = tokens // SPAN
    hops = width // HOP
    rows = n * STEPS
    requests = prompt_len.shape[0]
    hbm = pl.BlockSpec(memory_space=pltpu.HBM)
    vmem = pl.BlockSpec(memory_space=pltpu.VMEM)
    dma = pltpu.SemaphoreType.DMA
    slots = (n, STEPS)
    operands = (
        ssm_input, bmat, cmat, dt_raw.T, a_log[None, :], d_skip[None, :],
        prompt_len[None, :], owner[None, :], dec_x, dec_b, dec_c, dec_dt,
    )
    out, dout = pl.pallas_call(
        functools.partial(kernel, n),
        out_shape=(
            pltpu.VMEM((tokens, width), BF16),
            pltpu.VMEM((1,) + slots + (width,), BF16),
        ),
        in_specs=[hbm] * 12,
        out_specs=(vmem, vmem),
        scratch_shapes=[
            pltpu.VMEM((tokens, width), BF16),
            pltpu.VMEM((tokens, gn), BF16),
            pltpu.VMEM((tokens, gn), BF16),
            pltpu.VMEM((heads, tokens), BF16),
            pltpu.VMEM((1, heads), F32),
            pltpu.VMEM((1, heads), F32),
            pltpu.VMEM((1, requests), jnp.int32),
            pltpu.VMEM((1, requests), jnp.int32),
            pltpu.VMEM(slots + (width,), BF16),
            pltpu.VMEM(slots + (gn,), BF16),
            pltpu.VMEM(slots + (heads,), BF16),
            pltpu.VMEM((n,) + slots + (gn,), BF16),
            pltpu.VMEM((rows, width), F32),
            pltpu.VMEM((rows, gn), F32),
            pltpu.VMEM((rows, heads), F32),
            pltpu.VMEM((rows, gn), F32),
            pltpu.VMEM((rows, gn), F32),
            pltpu.VMEM((n * rows, gn), F32),
            pltpu.VMEM((heads, width), BF16),
            pltpu.VMEM((8, width), F32),
            pltpu.VMEM((max(spans - 1, 1), N, width), F32),
            pltpu.VMEM((N, width), F32),
            pltpu.VMEM((tokens, width), F32),
            pltpu.VMEM((hops, N, HOP), BF16),
            pltpu.VMEM((hops, N, HOP), BF16),
            pltpu.VMEM((rows, width), F32),
            pltpu.VMEM((rows, width), F32),
            pltpu.VMEM((rows, width), F32),
            pltpu.VMEM((n,) + slots + (width,), BF16),
            pltpu.VMEM((n,) + slots + (width,), BF16),
            pltpu.VMEM((PIECES, n, STEPS, width // PIECES), BF16),
            pltpu.VMEM((PIECES, n, STEPS, width // PIECES), BF16),
            pltpu.VMEM((n, 8, heads), F32),
            pltpu.VMEM((n, 8, heads), F32),
            pltpu.VMEM((n + 2, 2, rows, heads), BF16),
            dma((15,)),
            dma((hops,)),
            dma((hops,)),
            dma((n,)),
            dma((n,)),
            dma((n,)),
            dma((n,)),
            dma((n, n)),
            dma((n, n)),
            dma((PIECES, n)),
            dma((PIECES, n)),
            pltpu.SemaphoreType.REGULAR((n,)),
        ],
        compiler_params=pltpu.CompilerParams(
            collective_id=0, has_side_effects=True, vmem_limit_bytes=56 * 1024 * 1024
        ),
    )(*(pltpu.with_memory_space_constraint(operand, pltpu.HBM) for operand in operands))
    return pl.pallas_call(
        store,
        out_shape=(
            jax.ShapeDtypeStruct(out.shape, BF16),
            jax.ShapeDtypeStruct(dout.shape, BF16),
        ),
        in_specs=[vmem, vmem],
        out_specs=(hbm, hbm),
        scratch_shapes=[dma((2,))],
    )(
        pltpu.with_memory_space_constraint(out, pltpu.VMEM),
        pltpu.with_memory_space_constraint(dout, pltpu.VMEM),
    )


def solution(mesh):
    placed = (
        P(("grp", "seq"), "tp"),
        P(("grp", "seq"), "tp"),
        P(("grp", "seq"), "tp"),
        P(("grp", "seq"), "tp"),
        P("tp"),
        P("tp"),
        P("grp"),
        P("grp"),
        P(("grp", "seq"), None, None, "tp"),
        P(("grp", "seq"), None, None, "tp"),
        P(("grp", "seq"), None, None, "tp"),
        P(("grp", "seq"), None, None, "tp"),
    )
    return jax.shard_map(
        shards,
        mesh=mesh,
        in_specs=placed,
        out_specs=(P(("grp", "seq"), "tp"), P(("grp", "seq"), None, None, "tp")),
        check_vma=False,
    )
```

```python
import functools

import jax
import jax.numpy as jnp
from jax import lax
from jax.experimental import pallas as pl
from jax.experimental.pallas import tpu as pltpu
from jax.sharding import PartitionSpec as P

P_SIZE = 64
N = 128
SPAN = 128
STEPS = 4
LANES = 256
HOP = 128
PIECES = 1
EARLY = 6
AHEAD = 4
FEW = 8
MESH = pl.DeviceIdType.MESH
F32 = jnp.float32
BF16 = jnp.bfloat16
FAR = -1e30


def iota(shape, axis):
    return lax.broadcasted_iota(jnp.int32, shape, axis)


def dot(a, b):
    return jnp.dot(a, b, preferred_element_type=F32)


def dot_t(a, b):
    return lax.dot_general(a, b, (((1,), (1,)), ((), ())), preferred_element_type=F32)


def halves(value, count):
    pieces = []
    for _ in range(count):
        piece = value.astype(BF16)
        pieces.append(piece)
        value = value - piece.astype(F32)
    return pieces


def picked(selector, value, count=3):
    parts = [dot(selector, piece) for piece in halves(value, count)]
    return sum(parts[1:], parts[0])


def spread(pieces, expand):
    parts = [dot(piece, expand) for piece in pieces]
    return sum(parts[1:], parts[0])


def ones(mask):
    return jnp.where(mask, 1.0, 0.0).astype(BF16)


def softplus(value):
    return jnp.maximum(value, 0.0) + jnp.log1p(jnp.exp(-jnp.abs(value)))


def aligned(index):
    return index if isinstance(index, int) else pl.multiple_of(index, 8)


def each(count, body):
    if count <= 4:
        for i in range(count):
            body(i)
    else:

        def turn(i, carry):
            body(i)
            return carry

        lax.fori_loop(0, count, turn, 0)


def kernel(
    n,
    x_hbm, b_hbm, c_hbm, dt_hbm, alog_hbm, skip_hbm, len_hbm, own_hbm,
    dx_hbm, db_hbm, dc_hbm, ddt_hbm,
    out_ref, dout_ref,
    x_ref, b_ref, c_ref, dt_ref, alog_ref, skip_ref, len_ref, own_ref,
    dx_ref, db_ref, ddt_ref, queries,
    xd, bd, dtd, asked, asked_own, asked_all,
    expand_ref, row_ref, first, total, base, inbuf, outbuf,
    res, local, reached, gathered, grow, zbuf, zin, rbuf, rin, lgout, lgin, factor,
    load_sem, send_state, recv_state, send_query, recv_query,
    send_log, recv_log, send_z, recv_z, send_r, recv_r, here,
):
    me = lax.axis_index("seq")
    tokens, width = x_ref.shape
    heads = dt_ref.shape[0]
    groups = b_ref.shape[1] // N
    per_group = heads // groups
    spans = tokens // SPAN
    chunks = width // LANES
    heads_chunk = LANES // P_SIZE
    hops = width // HOP
    parts = LANES // HOP
    rows = n * STEPS
    middle = (me > 0) & (me < n - 1)
    ending = (me == 0) | (me == n - 1)

    def lanes(chunk):
        return slice(chunk * LANES, (chunk + 1) * LANES)

    barrier = pltpu.get_barrier_semaphore()

    def greet(q):
        @pl.when((q > me) | (q == me - 1))
        def _():
            pl.semaphore_signal(barrier, inc=1, device_id={"seq": q}, device_id_type=MESH)

    sources = [
        (dt_hbm, dt_ref),
        (alog_hbm, alog_ref),
        (b_hbm, b_ref),
        (dc_hbm.at[0], queries.at[me]),
    ]
    cuts = [0, LANES, 2 * LANES, 4 * LANES, width]
    for begin, end in zip(cuts[:-1], cuts[1:]):
        sources.append((x_hbm.at[:, begin:end], x_ref.at[:, begin:end]))
    sources += [
        (c_hbm, c_ref),
        (skip_hbm, skip_ref),
        (len_hbm, len_ref),
        (own_hbm, own_ref),
        (ddt_hbm.at[0], ddt_ref),
        (db_hbm.at[0], db_ref),
        (dx_hbm.at[0], dx_ref),
    ]
    loads = [
        pltpu.make_async_copy(source, landing, load_sem.at[k])
        for k, (source, landing) in enumerate(sources)
    ]
    for copy in loads[:5]:
        copy.start()
    each(n, greet)

    def push(source, landing, sends, recvs, target):
        return pltpu.make_async_remote_copy(
            src_ref=source, dst_ref=landing, send_sem=sends, recv_sem=recvs,
            device_id={"seq": target}, device_id_type=MESH,
        )

    def query(q, origin, s):
        return push(
            queries.at[origin, s], queries.at[origin, s],
            send_query.at[q, s], recv_query.at[origin, s], q,
        )

    def query_slots(q, origin, body):
        def turn(s):
            @pl.when((s == q) | ((s > q) & (q > origin)))
            def _():
                body(query(q, origin, s))

        if n <= FEW:
            each(n, turn)
        else:
            body(
                push(
                    queries.at[origin], queries.at[origin],
                    send_query.at[q, 0], recv_query.at[origin, 0], q,
                )
            )

    def log_to(q, origin):
        return push(lgout.at[q], lgin.at[origin], send_log.at[q], recv_log.at[origin], q)

    def z_to(q, origin, s):
        return push(
            zbuf.at[q, s], zin.at[origin, s], send_z.at[q, s], recv_z.at[origin, s], q
        )

    def slots_from(origin, body):
        def turn(s):
            @pl.when(s >= origin)
            def _():
                body(s)

        each(n, turn)

    def r_to(q, origin, piece):
        return push(
            rbuf.at[piece, q], rin.at[piece, origin],
            send_r.at[piece, q], recv_r.at[piece, origin], q,
        )

    def onward(hop):
        return push(
            outbuf.at[hop], inbuf.at[hop], send_state.at[hop], recv_state.at[hop],
            lax.rem(me + 1, n),
        )

    def entered():
        pl.semaphore_wait(barrier, me + jnp.where(me < n - 1, 1, 0))

    @pl.when(me >= 2)
    def _():
        entered()

        def announce(q):
            @pl.when(q < me - 1)
            def _():
                pl.semaphore_signal(here.at[me], inc=1, device_id={"seq": q}, device_id_type=MESH)

        each(n, announce)

    expand_ref[...] = ones(iota((heads, width), 0) == iota((heads, width), 1) // P_SIZE)
    t_row, t_col = iota((tokens, tokens), 0), iota((tokens, tokens), 1)
    upper = ones(((t_row // SPAN) == (t_col // SPAN)) & (t_col <= t_row))
    loads[0].wait()
    loads[1].wait()
    for copy in loads[5:]:
        copy.start()
    step_t = softplus(dt_ref[...].astype(F32))
    step = step_t.T
    rate = -jnp.exp(alog_ref[...])
    cum = picked(upper, rate * step)
    last = [cum[(s + 1) * SPAN - 1:(s + 1) * SPAN, :] for s in range(spans)]
    whole = sum(last[1:], last[0])
    into = jnp.concatenate(
        [
            jnp.exp(last[s] - cum[s * SPAN:(s + 1) * SPAN]) * step[s * SPAN:(s + 1) * SPAN]
            for s in range(spans)
        ],
        axis=0,
    )
    into_parts = halves(into, 2)
    grown = [halves(jnp.exp(last[s]), 2) for s in range(spans)]
    loads[2].wait()
    b_t = [
        [b_ref[s * SPAN:(s + 1) * SPAN, g * N:(g + 1) * N].T for g in range(groups)]
        for s in range(spans)
    ]

    def relay(hop, who):
        @pl.when(who)
        def _():
            onward(hop).wait_recv()
            at = slice(hop * HOP, (hop + 1) * HOP)
            outbuf[hop] = (row_ref[0:1, at] * inbuf[hop].astype(F32) + total[:, at]).astype(BF16)
            onward(hop).start()

    second = (me == 1) & (me < n - 1)
    later = (me > 1) & (me < n - 1)
    for chunk in range(chunks):
        if chunk * LANES in cuts:
            loads[4 + cuts.index(chunk * LANES)].wait()
        g = chunk * heads_chunk // per_group
        expand = expand_ref[:, lanes(chunk)]
        weighted = (x_ref[:, lanes(chunk)].astype(F32) * spread(into_parts, expand)).astype(BF16)
        state = None
        for s in range(spans):
            own = dot(b_t[s][g], weighted[s * SPAN:(s + 1) * SPAN])
            state = own if state is None else spread(grown[s], expand) * state + own
            if s < spans - 1:
                first[s, :, lanes(chunk)] = state
        total[:, lanes(chunk)] = state
        if chunk == 0:

            @pl.when(me < 2)
            def _():
                entered()

        @pl.when(me == 0)
        def _():
            for part in range(parts):
                hop = chunk * parts + part
                outbuf[hop] = state[:, part * HOP:(part + 1) * HOP].astype(BF16)
                if hop < EARLY:
                    onward(hop).start()

        if chunk == 0:
            loads[3].wait()

            def ask_near(q):
                @pl.when((q < me) | (q == me + 1))
                def _():
                    query_slots(q, me, lambda copy: copy.start())

            each(n, ask_near)
        if chunk == 3:
            for copy in loads[4 + len(cuts) - 1:]:
                copy.wait()
            row_kind = iota((8, heads), 0)
            row_value = jnp.where(
                row_kind == 0, jnp.exp(whole), jnp.where(row_kind == 1, skip_ref[...], jnp.exp(last[0]))
            )
            row_ref[...] = spread(halves(row_value, 3), expand_ref[...])
        if chunk > chunks - AHEAD:
            relay(chunk - chunks + AHEAD - 1, second)

    def ask_far(q):
        @pl.when(q > me + 1)
        def _():
            pl.semaphore_wait(here.at[q], 1)
            query_slots(q, me, lambda copy: copy.start())

    each(n, ask_far)

    @pl.when(me == 0)
    def _():
        for hop in range(EARLY, hops):
            onward(hop).start()


    outer_parts = halves(jnp.exp(cum), 2)
    cum_t = cum.T
    scores = []
    for s in range(spans):
        at = slice(s * SPAN, (s + 1) * SPAN)
        scores.append([])
        for g in range(groups):
            cols = slice(g * N, (g + 1) * N)
            scores[s].append(dot_t(c_ref[at, cols], b_ref[at, cols]))
    relay(AHEAD - 1, second)
    causal = iota((SPAN, SPAN), 0) >= iota((SPAN, SPAN), 1)
    low = ones(iota((1, 2 * P_SIZE), 1) < P_SIZE)
    high = ones(iota((1, 2 * P_SIZE), 1) >= P_SIZE)

    def pair_input(start, s):
        x_pair = x_ref[s * SPAN:(s + 1) * SPAN, start:start + 2 * P_SIZE]
        return jnp.concatenate([x_pair * low, x_pair * high], axis=0)

    def weights(head, s):
        at = slice(s * SPAN, (s + 1) * SPAN)
        gap = jnp.where(causal, cum[at, head:head + 1] - cum_t[head:head + 1, at], FAR)
        main = scores[s][head // per_group] * jnp.exp(gap) * step_t[head:head + 1, at]
        return main.astype(BF16)

    def inner(hop):
        head, start = hop * HOP // P_SIZE, hop * HOP
        for s in range(spans):
            at = slice(s * SPAN, (s + 1) * SPAN)
            left = jnp.concatenate([weights(head, s), weights(head + 1, s)], axis=1)
            skipped = row_ref[1:2, start:start + HOP] * x_ref[at, start:start + HOP].astype(F32)
            base[at, start:start + HOP] = dot(left, pair_input(start, s)) + skipped

    def asked_by_others():
        def take(q):
            @pl.when(q != me)
            def _():
                query_slots(me, q, lambda copy: copy.wait_recv())

        each(n, take)
        for s in range(n):
            asked[s * STEPS:(s + 1) * STEPS, :] = queries[s, me].astype(F32)

        def lay(q):
            found = jnp.concatenate([queries[q, s].astype(F32) for s in range(n)], axis=0)
            asked_all[pl.ds(aligned(q * rows), rows), :] = found

        each(n, lay)

    for s in range(n):
        asked_own[s * STEPS:(s + 1) * STEPS, :] = queries[me, s].astype(F32)
        xd[s * STEPS:(s + 1) * STEPS, :] = dx_ref[s].astype(F32)
        bd[s * STEPS:(s + 1) * STEPS, :] = db_ref[s].astype(F32)
        dtd[s * STEPS:(s + 1) * STEPS, :] = ddt_ref[s].astype(F32)

    requests = len_ref.shape[1]
    final = len_ref[...] - 1
    row_r = iota((rows, requests), 0) // STEPS
    here_now = (final >= me * tokens) & (final < (me + 1) * tokens)
    chosen = here_now & (own_ref[...] == row_r)
    spot = jnp.sum(jnp.where(chosen, final - me * tokens, 0), axis=1, keepdims=True)
    place = iota((rows, tokens), 1)
    upto = (place <= spot) & (place // SPAN == spot // SPAN)
    cum_spot = picked(ones(place == spot), cum)
    spot_span = spot // SPAN
    spot_parts = halves(jnp.exp(cum_spot), 2)
    reach = cum_spot
    for s in range(spans - 1):
        reach = reach + jnp.where(spot_span > s, last[s], 0.0)
    reach_parts = halves(jnp.exp(reach), 2)
    for q in range(n):
        lgout[q] = jnp.where(row_kind == 0, reach[q * STEPS:q * STEPS + 1], whole)

    def tell(q):
        @pl.when(q < me)
        def _():
            log_to(q, me).start()

    each(n, tell)

    wanted = (
        (own_ref[...] == me) & (final >= row_r * tokens) & (final < (row_r + 1) * tokens)
    )
    present = jnp.sum(jnp.where(wanted, 1, 0), axis=1, keepdims=True) > 0
    r_row, r_col = iota((rows, rows), 0), iota((rows, rows), 1)
    slot = (r_row // STEPS) == (r_col // STEPS)
    row_h = iota((rows, heads), 0)

    def owner_start():
        dstep = softplus(dtd[...])
        running = picked(ones(slot & (r_col <= r_row)), rate * dstep)
        c_own = asked_own[...].astype(BF16)
        b_own = bd[...].astype(BF16)
        head_group = iota((rows, heads), 1) // per_group
        pairs = [
            dot_t(c_own[:, g * N:(g + 1) * N], b_own[:, g * N:(g + 1) * N]) for g in range(groups)
        ]
        fresh_parts, fresh_pick = [], []
        for k in range(STEPS):
            chosen_k = slot & (r_col % STEPS == k)
            pick = ones(chosen_k)
            score = jnp.zeros((rows, heads), F32)
            for g in range(groups):
                value = jnp.sum(jnp.where(chosen_k, pairs[g], 0.0), axis=1, keepdims=True)
                score = jnp.where(head_group == g, value, score)
            gap = jnp.where(row_h % STEPS >= k, running - picked(pick, running), FAR)
            fresh_parts.append(halves(jnp.exp(gap) * picked(pick, dstep) * score, 2))
            fresh_pick.append(pick)
        return running, fresh_parts, fresh_pick

    def owner_part(chunk, fresh_parts, fresh_pick):
        expand = expand_ref[:, lanes(chunk)]
        xd_part = xd[:, lanes(chunk)]
        value = row_ref[1:2, lanes(chunk)] * xd_part
        for k in range(STEPS):
            value = value + spread(fresh_parts[k], expand) * dot(
                fresh_pick[k], xd_part.astype(BF16)
            )
        res[:, lanes(chunk)] = value

    def owner_factors(running):
        def heard(q):
            @pl.when(q > me)
            def _():
                log_to(me, q).wait_recv()

        each(n, heard)
        row_s = row_h // STEPS
        exponent = reach
        for s in range(n):
            exponent = jnp.where((row_s == s) & (s > me), lgin[s, 0:1, :], exponent)
        for q in reversed(range(n)):
            level = jnp.where(row_s > q, exponent, jnp.where(row_s == q, 0.0, FAR))
            for k, piece in enumerate(halves(jnp.exp(running + level), 2)):
                factor[q, k] = piece
            through = jnp.where(q > me, lgin[q, 1:2, :], jnp.where(q == me, whole, 0.0))
            exponent = exponent + jnp.where(row_s > q, through, 0.0)
        level = jnp.where(row_s > me, exponent, jnp.where(row_s == me, reach, FAR))
        for k, piece in enumerate(halves(jnp.exp(running + level), 2)):
            factor[n, k] = piece
        for k, piece in enumerate(halves(jnp.exp(running), 2)):
            factor[n + 1, k] = piece

    def scale(index, chunk):
        expand = expand_ref[:, lanes(chunk)]
        return dot(factor[index, 0], expand) + dot(factor[index, 1], expand)

    def source_scores():
        found = asked[...].astype(BF16)
        return [
            [
                dot_t(found[:, g * N:(g + 1) * N], b_ref[s * SPAN:(s + 1) * SPAN, g * N:(g + 1) * N])
                for g in range(groups)
            ]
            for s in range(spans)
        ]

    def source_part(chunk, dec_scores):
        g = chunk * heads_chunk // per_group
        cols = slice(g * N, (g + 1) * N)
        found = asked[:, cols].astype(BF16)
        expand = expand_ref[:, lanes(chunk)]
        side = []
        for part in range(parts):
            hop = chunk * parts + part
            head, start = hop * HOP // P_SIZE, hop * HOP
            value = None
            for s in range(spans):
                at = slice(s * SPAN, (s + 1) * SPAN)
                left = []
                for h in (head, head + 1):
                    gap = jnp.where(upto[:, at], cum_spot[:, h:h + 1] - cum_t[h:h + 1, at], FAR)
                    left.append(
                        (dec_scores[s][g] * jnp.exp(gap) * step_t[h:h + 1, at]).astype(BF16)
                    )
                more = dot(jnp.concatenate(left, axis=1), pair_input(start, s))
                value = more if value is None else value + more
            side.append(value)
        value = jnp.concatenate(side, axis=1)
        held = jnp.zeros((rows, LANES), F32)
        for s in range(1, spans):
            begun = dot(found, first[s - 1, :, lanes(chunk)].astype(BF16))
            held = jnp.where(spot_span == s, begun, held)
        value = value + spread(spot_parts, expand) * held
        local[:, lanes(chunk)] = value
        state = total[:, lanes(chunk)].astype(BF16)
        if n <= 4:
            everything = dot(asked_all[:, cols].astype(BF16), state)

        def lay(i):
            local_i = local[pl.ds(aligned(i * 2 * STEPS), 2 * STEPS), lanes(chunk)]
            for half in range(2):
                q = 2 * i + half
                if n <= 4:
                    found_q = everything[q * rows:(q + 1) * rows]
                else:
                    left = asked_all[pl.ds(aligned(q * rows), rows), cols]
                    found_q = dot(left.astype(BF16), state)
                for s in range(n):
                    zbuf[q, s, :, lanes(chunk)] = jnp.where(
                        me == s,
                        local_i[half * STEPS:(half + 1) * STEPS],
                        found_q[s * STEPS:(s + 1) * STEPS],
                    ).astype(BF16)

        each(n // 2, lay)

    def add_z(ref, q, chunk):
        value = jnp.concatenate([ref[q, s, :, lanes(chunk)].astype(F32) for s in range(n)], axis=0)
        kept = iota((rows, 1), 0) // STEPS >= q
        res[:, lanes(chunk)] += jnp.where(kept, scale(q, chunk) * value, 0.0)

    def arrived(begin, end):
        return jnp.concatenate([inbuf[h] for h in range(begin // HOP, end // HOP)], axis=1)

    def carry(begin, end, alone=False, before=None):
        g = begin // P_SIZE // per_group
        cols = slice(g * N, (g + 1) * N)
        area = slice(begin, end)
        expand = expand_ref[:, area]
        outer = spread(outer_parts, expand)
        if before is not None:
            before()
        if not alone:
            incoming = arrived(begin, end)
        for s in range(spans):
            at = slice(s * SPAN, (s + 1) * SPAN)
            if alone and s == 0:
                out_ref[at, area] = base[at, area].astype(BF16)
                continue
            if s == 0:
                held = incoming
                passed = None
            elif alone:
                held = first[s - 1, :, area].astype(BF16)
            else:
                step_on = row_ref[2:3, area] if s == 1 else spread(grown[s - 1], expand)
                passed = step_on if passed is None else passed * step_on
                held = (passed * incoming.astype(F32) + first[s - 1, :, area]).astype(BF16)
            out_ref[at, area] = (
                base[at, area] + outer[at] * dot(c_ref[at, cols], held)
            ).astype(BF16)

    def carry_requests(chunk, last=False):
        g = chunk * heads_chunk // per_group
        cols = slice(g * N, (g + 1) * N)
        left = jnp.concatenate([asked[:, cols], asked_own[:, cols]], axis=0).astype(BF16)
        carried = dot(left, arrived(chunk * LANES, (chunk + 1) * LANES))
        if not last:
            reached[:, lanes(chunk)] = (
                spread(reach_parts, expand_ref[:, lanes(chunk)]) * carried[:rows]
            )
        gathered[:, lanes(chunk)] = carried[rows:]

    def finish_requests(chunk):
        res[:, lanes(chunk)] += scale(n, chunk) * gathered[:, lanes(chunk)]

    def give(piece):
        wide = width // PIECES
        area = slice(piece * wide, (piece + 1) * wide)
        value = (reached[:, area] + local[:, area]).astype(BF16)
        for q in range(n):
            rbuf[piece, q] = value[q * STEPS:(q + 1) * STEPS]

        def hand(q):
            @pl.when(q > me)
            def _():
                r_to(q, me, piece).start()

        each(n, hand)

    def receive(piece):
        def take(q):
            @pl.when(q < me)
            def _():
                r_to(me, q, piece).wait_recv()

        each(n, take)
        wide = width // PIECES
        area = slice(piece * wide, (piece + 1) * wide)
        value = jnp.concatenate([rin[piece, q].astype(F32) for q in range(n)], axis=0)
        before = iota((rows, 1), 0) // STEPS < me
        res[:, area] += jnp.where(before, grow[:, area] * value, 0.0)

    def answer(q):
        @pl.when(q < me)
        def _():
            slots_from(me, lambda s: z_to(q, me, s).start())

    half = hops // 2
    kept = {}
    for hop in range(hops):
        inner(hop)
        if hop + AHEAD < hops:
            relay(hop + AHEAD, second)
        relay(hop, later)
        chunk = hop // parts
        if hop % parts == parts - 1:
            if chunk == chunks - 1:

                @pl.when(later)
                def _():
                    carry_requests(chunk)
                    for piece in range(PIECES):
                        give(piece)

            @pl.when(middle)
            def _():
                carry(chunk * LANES, (chunk + 1) * LANES)

        if hop == 3:
            asked_by_others()
            kept["scores"] = source_scores()
        if 4 <= hop < 8:
            for more in range((hop - 4) * chunks // 4, (hop - 3) * chunks // 4):
                source_part(more, kept["scores"])
        if hop == 7:
            each(n, answer)
        if 8 <= hop < hops - 1:

            @pl.when(middle)
            def _():
                carry_requests(hop - 8)

    @pl.when(second)
    def _():
        carry_requests(chunks - 1)

    @pl.when(me == 0)
    def _():
        reached[...] = jnp.zeros(reached.shape, F32)

    @pl.when((me == 0) | second)
    def _():
        for piece in range(PIECES):
            give(piece)

    running, fresh_parts, fresh_pick = owner_start()
    owner_factors(running)
    for chunk in range(chunks):
        owner_part(chunk, fresh_parts, fresh_pick)
        add_z(zbuf, me, chunk)
        grow[:, lanes(chunk)] = scale(n + 1, chunk)

    @pl.when(middle)
    def _():
        for chunk in range(chunks):
            finish_requests(chunk)

    @pl.when(me == n - 1)
    def _():
        for chunk in range(chunks):
            arrivals = [onward(chunk * parts + part).wait_recv for part in range(parts)]
            if chunk == chunks - 1:
                for part in range(parts):
                    begin = (chunk * parts + part) * HOP
                    carry(begin, begin + HOP, before=arrivals[part])
            else:
                carry(
                    chunk * LANES, (chunk + 1) * LANES,
                    before=lambda: [arrival() for arrival in arrivals],
                )
            carry_requests(chunk, last=True)
            finish_requests(chunk)
        for piece in range(PIECES):
            receive(piece)

    @pl.when(me == 0)
    def _():
        for chunk in range(chunks):
            carry(chunk * LANES, (chunk + 1) * LANES, alone=True)

    def collect(q):
        @pl.when(q > me)
        def _():
            slots_from(q, lambda s: z_to(me, q, s).wait_recv())
            for chunk in range(chunks):
                add_z(zin, q, chunk)

    each(n, collect)


    @pl.when(middle)
    def _():
        for piece in range(PIECES):
            receive(piece)

    done = jnp.where(present, res[...], 0.0).astype(BF16)
    for s in range(n):
        dout_ref[0, s] = done[s * STEPS:(s + 1) * STEPS]

    @pl.when(me < n - 1)
    def _():
        for hop in range(hops):
            onward(hop).wait_send()

    def finish(q):
        @pl.when(q != me)
        def _():
            query_slots(q, me, lambda copy: copy.wait_send())

        @pl.when(q < me)
        def _():
            log_to(q, me).wait_send()
            slots_from(me, lambda s: z_to(q, me, s).wait_send())

        @pl.when(q > me)
        def _():
            for piece in range(PIECES):
                r_to(q, me, piece).wait_send()

    each(n, finish)


def store(out_vmem, dout_vmem, out_hbm, dout_hbm, sem):
    copies = [
        pltpu.make_async_copy(out_vmem, out_hbm, sem.at[0]),
        pltpu.make_async_copy(dout_vmem, dout_hbm, sem.at[1]),
    ]
    for copy in copies:
        copy.start()
    for copy in copies:
        copy.wait()


def shards(
    ssm_input, bmat, cmat, dt_raw, a_log, d_skip, prompt_len, owner, dec_x, dec_b, dec_c, dec_dt
):
    n = lax.axis_size("seq")
    tokens, width = ssm_input.shape
    heads = dt_raw.shape[1]
    gn = bmat.shape[1]
    spans = tokens // SPAN
    hops = width // HOP
    rows = n * STEPS
    requests = prompt_len.shape[0]
    hbm = pl.BlockSpec(memory_space=pltpu.HBM)
    vmem = pl.BlockSpec(memory_space=pltpu.VMEM)
    dma = pltpu.SemaphoreType.DMA
    slots = (n, STEPS)
    operands = (
        ssm_input, bmat, cmat, dt_raw.T, a_log[None, :], d_skip[None, :],
        prompt_len[None, :], owner[None, :], dec_x, dec_b, dec_c, dec_dt,
    )
    out, dout = pl.pallas_call(
        functools.partial(kernel, n),
        out_shape=(
            pltpu.VMEM((tokens, width), BF16),
            pltpu.VMEM((1,) + slots + (width,), BF16),
        ),
        in_specs=[hbm] * 12,
        out_specs=(vmem, vmem),
        scratch_shapes=[
            pltpu.VMEM((tokens, width), BF16),
            pltpu.VMEM((tokens, gn), BF16),
            pltpu.VMEM((tokens, gn), BF16),
            pltpu.VMEM((heads, tokens), BF16),
            pltpu.VMEM((1, heads), F32),
            pltpu.VMEM((1, heads), F32),
            pltpu.VMEM((1, requests), jnp.int32),
            pltpu.VMEM((1, requests), jnp.int32),
            pltpu.VMEM(slots + (width,), BF16),
            pltpu.VMEM(slots + (gn,), BF16),
            pltpu.VMEM(slots + (heads,), BF16),
            pltpu.VMEM((n,) + slots + (gn,), BF16),
            pltpu.VMEM((rows, width), F32),
            pltpu.VMEM((rows, gn), F32),
            pltpu.VMEM((rows, heads), F32),
            pltpu.VMEM((rows, gn), F32),
            pltpu.VMEM((rows, gn), F32),
            pltpu.VMEM((n * rows, gn), F32),
            pltpu.VMEM((heads, width), BF16),
            pltpu.VMEM((8, width), F32),
            pltpu.VMEM((max(spans - 1, 1), N, width), F32),
            pltpu.VMEM((N, width), F32),
            pltpu.VMEM((tokens, width), F32),
            pltpu.VMEM((hops, N, HOP), BF16),
            pltpu.VMEM((hops, N, HOP), BF16),
            pltpu.VMEM((rows, width), F32),
            pltpu.VMEM((rows, width), F32),
            pltpu.VMEM((rows, width), F32),
            pltpu.VMEM((rows, width), F32),
            pltpu.VMEM((rows, width), F32),
            pltpu.VMEM((n,) + slots + (width,), BF16),
            pltpu.VMEM((n,) + slots + (width,), BF16),
            pltpu.VMEM((PIECES, n, STEPS, width // PIECES), BF16),
            pltpu.VMEM((PIECES, n, STEPS, width // PIECES), BF16),
            pltpu.VMEM((n, 8, heads), F32),
            pltpu.VMEM((n, 8, heads), F32),
            pltpu.VMEM((n + 2, 2, rows, heads), BF16),
            dma((15,)),
            dma((hops,)),
            dma((hops,)),
            dma((n, n if n <= FEW else 1)),
            dma((n, n if n <= FEW else 1)),
            dma((n,)),
            dma((n,)),
            dma((n, n)),
            dma((n, n)),
            dma((PIECES, n)),
            dma((PIECES, n)),
            pltpu.SemaphoreType.REGULAR((n,)),
        ],
        compiler_params=pltpu.CompilerParams(
            collective_id=0, has_side_effects=True, vmem_limit_bytes=61 * 1024 * 1024
        ),
    )(*(pltpu.with_memory_space_constraint(operand, pltpu.HBM) for operand in operands))
    return pl.pallas_call(
        store,
        out_shape=(
            jax.ShapeDtypeStruct(out.shape, BF16),
            jax.ShapeDtypeStruct(dout.shape, BF16),
        ),
        in_specs=[vmem, vmem],
        out_specs=(hbm, hbm),
        scratch_shapes=[dma((2,))],
    )(
        pltpu.with_memory_space_constraint(out, pltpu.VMEM),
        pltpu.with_memory_space_constraint(dout, pltpu.VMEM),
    )


def solution(mesh):
    placed = (
        P(("grp", "seq"), "tp"),
        P(("grp", "seq"), "tp"),
        P(("grp", "seq"), "tp"),
        P(("grp", "seq"), "tp"),
        P("tp"),
        P("tp"),
        P("grp"),
        P("grp"),
        P(("grp", "seq"), None, None, "tp"),
        P(("grp", "seq"), None, None, "tp"),
        P(("grp", "seq"), None, None, "tp"),
        P(("grp", "seq"), None, None, "tp"),
    )
    return jax.shard_map(
        shards,
        mesh=mesh,
        in_specs=placed,
        out_specs=(P(("grp", "seq"), "tp"), P(("grp", "seq"), None, None, "tp")),
        check_vma=False,
    )
```

```python
import functools

import jax
import jax.numpy as jnp
from jax import lax
from jax.experimental import pallas as pl
from jax.experimental.pallas import tpu as pltpu
from jax.sharding import PartitionSpec as P

P_SIZE = 64
N = 128
SPAN = 128
STEPS = 4
LANES = 256
HOP = 128
PIECES = 1
EARLY = 6
AHEAD = 4
FEW = 8
MESH = pl.DeviceIdType.MESH
F32 = jnp.float32
BF16 = jnp.bfloat16
FAR = -1e30


def iota(shape, axis):
    return lax.broadcasted_iota(jnp.int32, shape, axis)


def dot(a, b):
    return jnp.dot(a, b, preferred_element_type=F32)


def dot_t(a, b):
    return lax.dot_general(a, b, (((1,), (1,)), ((), ())), preferred_element_type=F32)


def halves(value, count):
    pieces = []
    for _ in range(count):
        piece = value.astype(BF16)
        pieces.append(piece)
        value = value - piece.astype(F32)
    return pieces


def picked(selector, value, count=3):
    parts = [dot(selector, piece) for piece in halves(value, count)]
    return sum(parts[1:], parts[0])


def spread(pieces, expand):
    parts = [dot(piece, expand) for piece in pieces]
    return sum(parts[1:], parts[0])


def ones(mask):
    return jnp.where(mask, 1.0, 0.0).astype(BF16)


def softplus(value):
    return jnp.maximum(value, 0.0) + jnp.log1p(jnp.exp(-jnp.abs(value)))


def aligned(index):
    return index if isinstance(index, int) else pl.multiple_of(index, 8)


def each(count, body):
    if count <= 4:
        for i in range(count):
            body(i)
    else:

        def turn(i, carry):
            body(i)
            return carry

        lax.fori_loop(0, count, turn, 0)


def kernel(
    n,
    x_hbm, b_hbm, c_hbm, dt_hbm, alog_hbm, skip_hbm, len_hbm, own_hbm,
    dx_hbm, db_hbm, dc_hbm, ddt_hbm,
    out_ref, dout_ref,
    x_ref, b_ref, c_ref, dt_ref, alog_ref, skip_ref, len_ref, own_ref,
    dx_ref, db_ref, ddt_ref, queries,
    xd, bd, dtd, asked, asked_own, asked_all,
    expand_ref, row_ref, first, total, base, inbuf, outbuf,
    res, local, reached, gathered, grow, zbuf, zin, rbuf, rin, lgout, lgin, factor,
    load_sem, send_state, recv_state, send_query, recv_query,
    send_log, recv_log, send_z, recv_z, send_r, recv_r, here,
):
    me = lax.axis_index("seq")
    core = lax.rem(lax.axis_index("tp"), 2)
    tokens, width = x_ref.shape
    heads = dt_ref.shape[0]
    groups = b_ref.shape[1] // N
    per_group = heads // groups
    spans = tokens // SPAN
    chunks = width // LANES
    heads_chunk = LANES // P_SIZE
    hops = width // HOP
    parts = LANES // HOP
    rows = n * STEPS
    middle = (me > 0) & (me < n - 1)
    ending = (me == 0) | (me == n - 1)

    def lanes(chunk):
        return slice(chunk * LANES, (chunk + 1) * LANES)

    barrier = pltpu.get_barrier_semaphore()

    def greet(q):
        @pl.when((q > me) | (q == me - 1))
        def _():
            pl.semaphore_signal(barrier, inc=1, device_id={"seq": q}, device_id_type=MESH)

    sources = [
        (dt_hbm, dt_ref),
        (alog_hbm, alog_ref),
        (b_hbm, b_ref),
        (dc_hbm.at[0], queries.at[me]),
    ]
    cuts = [0, LANES, 2 * LANES, 4 * LANES, width]
    for begin, end in zip(cuts[:-1], cuts[1:]):
        sources.append((x_hbm.at[:, begin:end], x_ref.at[:, begin:end]))
    sources += [
        (c_hbm, c_ref),
        (skip_hbm, skip_ref),
        (len_hbm, len_ref),
        (own_hbm, own_ref),
        (ddt_hbm.at[0], ddt_ref),
        (db_hbm.at[0], db_ref),
        (dx_hbm.at[0], dx_ref),
    ]
    loads = [
        pltpu.make_async_copy(source, landing, load_sem.at[k])
        for k, (source, landing) in enumerate(sources)
    ]
    for copy in loads[:5]:
        copy.start()
    each(n, greet)

    def push(source, landing, sends, recvs, target):
        return pltpu.make_async_remote_copy(
            src_ref=source, dst_ref=landing, send_sem=sends, recv_sem=recvs,
            device_id={"seq": target}, device_id_type=MESH,
        )

    def query(q, origin, s):
        return push(
            queries.at[origin, s], queries.at[origin, s],
            send_query.at[q, s], recv_query.at[origin, s], q,
        )

    def query_slots(q, origin, body):
        def turn(s):
            @pl.when((s == q) | ((s > q) & (q > origin)))
            def _():
                body(query(q, origin, s))

        if n <= FEW:
            each(n, turn)
        else:
            body(
                push(
                    queries.at[origin], queries.at[origin],
                    send_query.at[q, 0], recv_query.at[origin, 0], q,
                )
            )

    def log_to(q, origin):
        return push(lgout.at[q], lgin.at[origin], send_log.at[q], recv_log.at[origin], q)

    def z_to(q, origin, s):
        return push(
            zbuf.at[q, s], zin.at[origin, s], send_z.at[q, s], recv_z.at[origin, s], q
        )

    def slots_from(origin, body):
        def turn(s):
            @pl.when(s >= origin)
            def _():
                body(s)

        each(n, turn)

    def r_to(q, origin, piece):
        return push(
            rbuf.at[piece, q], rin.at[piece, origin],
            send_r.at[piece, q], recv_r.at[piece, origin], q,
        )

    def onward(hop):
        return push(
            outbuf.at[hop], inbuf.at[hop], send_state.at[hop], recv_state.at[hop],
            lax.rem(me + 1, n),
        )

    def entered():
        pl.semaphore_wait(barrier, me + jnp.where(me < n - 1, 1, 0))

    @pl.when(me >= 2)
    def _():
        entered()

        def announce(q):
            @pl.when(q < me - 1)
            def _():
                pl.semaphore_signal(here.at[me], inc=1, device_id={"seq": q}, device_id_type=MESH)

        each(n, announce)

    expand_ref[...] = ones(iota((heads, width), 0) == iota((heads, width), 1) // P_SIZE)
    t_row, t_col = iota((tokens, tokens), 0), iota((tokens, tokens), 1)
    upper = ones(((t_row // SPAN) == (t_col // SPAN)) & (t_col <= t_row))
    loads[0].wait()
    loads[1].wait()
    for copy in loads[5:]:
        copy.start()
    step_t = softplus(dt_ref[...].astype(F32))
    step = step_t.T
    rate = -jnp.exp(alog_ref[...])
    cum = picked(upper, rate * step)
    last = [cum[(s + 1) * SPAN - 1:(s + 1) * SPAN, :] for s in range(spans)]
    whole = sum(last[1:], last[0])
    into = jnp.concatenate(
        [
            jnp.exp(last[s] - cum[s * SPAN:(s + 1) * SPAN]) * step[s * SPAN:(s + 1) * SPAN]
            for s in range(spans)
        ],
        axis=0,
    )
    into_parts = halves(into, 2)
    grown = [halves(jnp.exp(last[s]), 2) for s in range(spans)]
    loads[2].wait()
    b_t = [
        [b_ref[s * SPAN:(s + 1) * SPAN, g * N:(g + 1) * N].T for g in range(groups)]
        for s in range(spans)
    ]

    def relay(hop, who):
        @pl.when(who)
        def _():
            onward(hop).wait_recv()
            at = slice(hop * HOP, (hop + 1) * HOP)
            outbuf[hop] = (row_ref[0:1, at] * inbuf[hop].astype(F32) + total[:, at]).astype(BF16)
            onward(hop).start()

    second = (me == 1) & (me < n - 1)
    later = (me > 1) & (me < n - 1)
    for chunk in range(chunks):
        if chunk * LANES in cuts:
            loads[4 + cuts.index(chunk * LANES)].wait()
        g = chunk * heads_chunk // per_group
        expand = expand_ref[:, lanes(chunk)]
        weighted = (x_ref[:, lanes(chunk)].astype(F32) * spread(into_parts, expand)).astype(BF16)
        state = None
        for s in range(spans):
            own = dot(b_t[s][g], weighted[s * SPAN:(s + 1) * SPAN])
            state = own if state is None else spread(grown[s], expand) * state + own
            if s < spans - 1:
                first[s, :, lanes(chunk)] = state
        total[:, lanes(chunk)] = state
        if chunk == 0:

            @pl.when(me < 2)
            def _():
                entered()

        @pl.when(me == 0)
        def _():
            for part in range(parts):
                hop = chunk * parts + part
                outbuf[hop] = state[:, part * HOP:(part + 1) * HOP].astype(BF16)
                if hop < EARLY:
                    onward(hop).start()

        if chunk == 0:
            loads[3].wait()

            def ask_near(q):
                @pl.when((q < me) | (q == me + 1))
                def _():
                    query_slots(q, me, lambda copy: copy.start())

            each(n, ask_near)
        if chunk == 3:
            for copy in loads[4 + len(cuts) - 1:]:
                copy.wait()
            row_kind = iota((8, heads), 0)
            row_value = jnp.where(
                row_kind == 0, jnp.exp(whole), jnp.where(row_kind == 1, skip_ref[...], jnp.exp(last[0]))
            )
            row_ref[...] = spread(halves(row_value, 3), expand_ref[...])
        if chunk > chunks - AHEAD:
            relay(chunk - chunks + AHEAD - 1, second)

    def ask_far(q):
        @pl.when(q > me + 1)
        def _():
            pl.semaphore_wait(here.at[q], 1)
            query_slots(q, me, lambda copy: copy.start())

    each(n, ask_far)

    @pl.when(me == 0)
    def _():
        for hop in range(EARLY, hops):
            onward(hop).start()


    outer_parts = halves(jnp.exp(cum), 2)
    cum_t = cum.T
    scores = []
    for s in range(spans):
        at = slice(s * SPAN, (s + 1) * SPAN)
        scores.append([])
        for g in range(groups):
            cols = slice(g * N, (g + 1) * N)
            scores[s].append(dot_t(c_ref[at, cols], b_ref[at, cols]))
    relay(AHEAD - 1, second)
    causal = iota((SPAN, SPAN), 0) >= iota((SPAN, SPAN), 1)
    low = ones(iota((1, 2 * P_SIZE), 1) < P_SIZE)
    high = ones(iota((1, 2 * P_SIZE), 1) >= P_SIZE)

    def pair_input(start, s):
        x_pair = x_ref[s * SPAN:(s + 1) * SPAN, start:start + 2 * P_SIZE]
        return jnp.concatenate([x_pair * low, x_pair * high], axis=0)

    def weights(head, s):
        at = slice(s * SPAN, (s + 1) * SPAN)
        gap = jnp.where(causal, cum[at, head:head + 1] - cum_t[head:head + 1, at], FAR)
        main = scores[s][head // per_group] * jnp.exp(gap) * step_t[head:head + 1, at]
        return main.astype(BF16)

    def inner(hop):
        head, start = hop * HOP // P_SIZE, hop * HOP
        for s in range(spans):
            at = slice(s * SPAN, (s + 1) * SPAN)
            left = jnp.concatenate([weights(head, s), weights(head + 1, s)], axis=1)
            skipped = row_ref[1:2, start:start + HOP] * x_ref[at, start:start + HOP].astype(F32)
            base[at, start:start + HOP] = dot(left, pair_input(start, s)) + skipped

    def asked_by_others():
        def take(q):
            @pl.when(q != me)
            def _():
                query_slots(me, q, lambda copy: copy.wait_recv())

        each(n, take)
        for s in range(n):
            asked[s * STEPS:(s + 1) * STEPS, :] = queries[s, me].astype(F32)

        def lay(q):
            found = jnp.concatenate([queries[q, s].astype(F32) for s in range(n)], axis=0)
            asked_all[pl.ds(aligned(q * rows), rows), :] = found

        each(n, lay)

    for s in range(n):
        asked_own[s * STEPS:(s + 1) * STEPS, :] = queries[me, s].astype(F32)
        xd[s * STEPS:(s + 1) * STEPS, :] = dx_ref[s].astype(F32)
        bd[s * STEPS:(s + 1) * STEPS, :] = db_ref[s].astype(F32)
        dtd[s * STEPS:(s + 1) * STEPS, :] = ddt_ref[s].astype(F32)

    requests = len_ref.shape[1]
    final = len_ref[...] - 1
    row_r = iota((rows, requests), 0) // STEPS
    here_now = (final >= me * tokens) & (final < (me + 1) * tokens)
    chosen = here_now & (own_ref[...] == row_r)
    spot = jnp.sum(jnp.where(chosen, final - me * tokens, 0), axis=1, keepdims=True)
    place = iota((rows, tokens), 1)
    upto = (place <= spot) & (place // SPAN == spot // SPAN)
    cum_spot = picked(ones(place == spot), cum)
    spot_span = spot // SPAN
    spot_parts = halves(jnp.exp(cum_spot), 2)
    reach = cum_spot
    for s in range(spans - 1):
        reach = reach + jnp.where(spot_span > s, last[s], 0.0)
    reach_parts = halves(jnp.exp(reach), 2)
    for q in range(n):
        lgout[q] = jnp.where(row_kind == 0, reach[q * STEPS:q * STEPS + 1], whole)

    def tell(q):
        @pl.when(q < me)
        def _():
            log_to(q, me).start()

    each(n, tell)

    wanted = (
        (own_ref[...] == me) & (final >= row_r * tokens) & (final < (row_r + 1) * tokens)
    )
    present = jnp.sum(jnp.where(wanted, 1, 0), axis=1, keepdims=True) > 0
    r_row, r_col = iota((rows, rows), 0), iota((rows, rows), 1)
    slot = (r_row // STEPS) == (r_col // STEPS)
    row_h = iota((rows, heads), 0)

    def owner_start():
        dstep = softplus(dtd[...])
        running = picked(ones(slot & (r_col <= r_row)), rate * dstep)
        c_own = asked_own[...].astype(BF16)
        b_own = bd[...].astype(BF16)
        head_group = iota((rows, heads), 1) // per_group
        pairs = [
            dot_t(c_own[:, g * N:(g + 1) * N], b_own[:, g * N:(g + 1) * N]) for g in range(groups)
        ]
        fresh_parts, fresh_pick = [], []
        for k in range(STEPS):
            chosen_k = slot & (r_col % STEPS == k)
            pick = ones(chosen_k)
            score = jnp.zeros((rows, heads), F32)
            for g in range(groups):
                value = jnp.sum(jnp.where(chosen_k, pairs[g], 0.0), axis=1, keepdims=True)
                score = jnp.where(head_group == g, value, score)
            gap = jnp.where(row_h % STEPS >= k, running - picked(pick, running), FAR)
            fresh_parts.append(halves(jnp.exp(gap) * picked(pick, dstep) * score, 2))
            fresh_pick.append(pick)
        return running, fresh_parts, fresh_pick

    def owner_part(chunk, fresh_parts, fresh_pick):
        expand = expand_ref[:, lanes(chunk)]
        xd_part = xd[:, lanes(chunk)]
        value = row_ref[1:2, lanes(chunk)] * xd_part
        for k in range(STEPS):
            value = value + spread(fresh_parts[k], expand) * dot(
                fresh_pick[k], xd_part.astype(BF16)
            )
        res[:, lanes(chunk)] = value

    def owner_factors(running):
        def heard(q):
            @pl.when(q > me)
            def _():
                log_to(me, q).wait_recv()

        each(n, heard)
        row_s = row_h // STEPS
        exponent = reach
        for s in range(n):
            exponent = jnp.where((row_s == s) & (s > me), lgin[s, 0:1, :], exponent)
        for q in reversed(range(n)):
            level = jnp.where(row_s > q, exponent, jnp.where(row_s == q, 0.0, FAR))
            for k, piece in enumerate(halves(jnp.exp(running + level), 2)):
                factor[q, k] = piece
            through = jnp.where(q > me, lgin[q, 1:2, :], jnp.where(q == me, whole, 0.0))
            exponent = exponent + jnp.where(row_s > q, through, 0.0)
        level = jnp.where(row_s > me, exponent, jnp.where(row_s == me, reach, FAR))
        for k, piece in enumerate(halves(jnp.exp(running + level), 2)):
            factor[n, k] = piece
        for k, piece in enumerate(halves(jnp.exp(running), 2)):
            factor[n + 1, k] = piece

    def scale(index, chunk):
        expand = expand_ref[:, lanes(chunk)]
        return dot(factor[index, 0], expand) + dot(factor[index, 1], expand)

    def source_scores():
        found = asked[...].astype(BF16)
        return [
            [
                dot_t(found[:, g * N:(g + 1) * N], b_ref[s * SPAN:(s + 1) * SPAN, g * N:(g + 1) * N])
                for g in range(groups)
            ]
            for s in range(spans)
        ]

    def source_part(chunk, dec_scores):
        g = chunk * heads_chunk // per_group
        cols = slice(g * N, (g + 1) * N)
        found = asked[:, cols].astype(BF16)
        expand = expand_ref[:, lanes(chunk)]
        side = []
        for part in range(parts):
            hop = chunk * parts + part
            head, start = hop * HOP // P_SIZE, hop * HOP
            value = None
            for s in range(spans):
                at = slice(s * SPAN, (s + 1) * SPAN)
                left = []
                for h in (head, head + 1):
                    gap = jnp.where(upto[:, at], cum_spot[:, h:h + 1] - cum_t[h:h + 1, at], FAR)
                    left.append(
                        (dec_scores[s][g] * jnp.exp(gap) * step_t[h:h + 1, at]).astype(BF16)
                    )
                more = dot(jnp.concatenate(left, axis=1), pair_input(start, s))
                value = more if value is None else value + more
            side.append(value)
        value = jnp.concatenate(side, axis=1)
        held = jnp.zeros((rows, LANES), F32)
        for s in range(1, spans):
            begun = dot(found, first[s - 1, :, lanes(chunk)].astype(BF16))
            held = jnp.where(spot_span == s, begun, held)
        value = value + spread(spot_parts, expand) * held
        local[:, lanes(chunk)] = value
        state = total[:, lanes(chunk)].astype(BF16)
        if n <= 4:
            everything = dot(asked_all[:, cols].astype(BF16), state)

        def lay(i):
            local_i = local[pl.ds(aligned(i * 2 * STEPS), 2 * STEPS), lanes(chunk)]
            for half in range(2):
                q = 2 * i + half
                if n <= 4:
                    found_q = everything[q * rows:(q + 1) * rows]
                else:
                    left = asked_all[pl.ds(aligned(q * rows), rows), cols]
                    found_q = dot(left.astype(BF16), state)
                for s in range(n):
                    zbuf[q, s, :, lanes(chunk)] = jnp.where(
                        me == s,
                        local_i[half * STEPS:(half + 1) * STEPS],
                        found_q[s * STEPS:(s + 1) * STEPS],
                    ).astype(BF16)

        each(n // 2, lay)

    def add_z(ref, q, chunk):
        value = jnp.concatenate([ref[q, s, :, lanes(chunk)].astype(F32) for s in range(n)], axis=0)
        kept = iota((rows, 1), 0) // STEPS >= q
        res[:, lanes(chunk)] += jnp.where(kept, scale(q, chunk) * value, 0.0)

    def arrived(begin, end):
        return jnp.concatenate([inbuf[h] for h in range(begin // HOP, end // HOP)], axis=1)

    def carry(begin, end, alone=False, before=None):
        g = begin // P_SIZE // per_group
        cols = slice(g * N, (g + 1) * N)
        area = slice(begin, end)
        expand = expand_ref[:, area]
        outer = spread(outer_parts, expand)
        if before is not None:
            before()
        if not alone:
            incoming = arrived(begin, end)
        for s in range(spans):
            at = slice(s * SPAN, (s + 1) * SPAN)
            if alone and s == 0:
                out_ref[at, area] = base[at, area].astype(BF16)
                continue
            if s == 0:
                held = incoming
                passed = None
            elif alone:
                held = first[s - 1, :, area].astype(BF16)
            else:
                step_on = row_ref[2:3, area] if s == 1 else spread(grown[s - 1], expand)
                passed = step_on if passed is None else passed * step_on
                held = (passed * incoming.astype(F32) + first[s - 1, :, area]).astype(BF16)
            out_ref[at, area] = (
                base[at, area] + outer[at] * dot(c_ref[at, cols], held)
            ).astype(BF16)

    def carry_requests(chunk, last=False):
        g = chunk * heads_chunk // per_group
        cols = slice(g * N, (g + 1) * N)
        left = jnp.concatenate([asked[:, cols], asked_own[:, cols]], axis=0).astype(BF16)
        carried = dot(left, arrived(chunk * LANES, (chunk + 1) * LANES))
        if not last:
            reached[:, lanes(chunk)] = (
                spread(reach_parts, expand_ref[:, lanes(chunk)]) * carried[:rows]
            )
        gathered[:, lanes(chunk)] = carried[rows:]

    def finish_requests(chunk):
        res[:, lanes(chunk)] += scale(n, chunk) * gathered[:, lanes(chunk)]

    def give(piece):
        wide = width // PIECES
        area = slice(piece * wide, (piece + 1) * wide)
        value = (reached[:, area] + local[:, area]).astype(BF16)
        for q in range(n):
            rbuf[piece, q] = value[q * STEPS:(q + 1) * STEPS]

        def hand(q):
            @pl.when(q > me)
            def _():
                r_to(q, me, piece).start()

        each(n, hand)

    def receive(piece):
        def take(q):
            @pl.when(q < me)
            def _():
                r_to(me, q, piece).wait_recv()

        each(n, take)
        wide = width // PIECES
        area = slice(piece * wide, (piece + 1) * wide)
        value = jnp.concatenate([rin[piece, q].astype(F32) for q in range(n)], axis=0)
        before = iota((rows, 1), 0) // STEPS < me
        res[:, area] += jnp.where(before, grow[:, area] * value, 0.0)

    def answer(q):
        @pl.when(q < me)
        def _():
            slots_from(me, lambda s: z_to(q, me, s).start())

    half = hops // 2
    kept = {}
    for hop in range(hops):
        inner(hop)
        if hop + AHEAD < hops:
            relay(hop + AHEAD, second)
        relay(hop, later)
        chunk = hop // parts
        if hop % parts == parts - 1:
            if chunk == chunks - 1:

                @pl.when(later)
                def _():
                    carry_requests(chunk)
                    for piece in range(PIECES):
                        give(piece)

            @pl.when(middle)
            def _():
                carry(chunk * LANES, (chunk + 1) * LANES)

        if hop == 3:
            asked_by_others()
            kept["scores"] = source_scores()
        if 4 <= hop < 8:
            for more in range((hop - 4) * chunks // 4, (hop - 3) * chunks // 4):
                source_part(more, kept["scores"])
        if hop == 7:
            each(n, answer)
        if hop == 8:

            @pl.when((me == 0) & (core == 0))
            def _():
                reached[...] = jnp.zeros(reached.shape, F32)
                for piece in range(PIECES):
                    give(piece)

        if 8 <= hop < hops - 1:

            @pl.when(middle)
            def _():
                carry_requests(hop - 8)

    @pl.when(second)
    def _():
        carry_requests(chunks - 1)

    @pl.when(me == 0)
    def _():
        reached[...] = jnp.zeros(reached.shape, F32)

    @pl.when(second & (core == 0))
    def _():
        for piece in range(PIECES):
            give(piece)

    running, fresh_parts, fresh_pick = owner_start()
    owner_factors(running)
    for chunk in range(chunks):
        owner_part(chunk, fresh_parts, fresh_pick)
        add_z(zbuf, me, chunk)
        grow[:, lanes(chunk)] = scale(n + 1, chunk)

    @pl.when(middle)
    def _():
        for chunk in range(chunks):
            finish_requests(chunk)

    @pl.when(me == n - 1)
    def _():
        for chunk in range(chunks):
            arrivals = [onward(chunk * parts + part).wait_recv for part in range(parts)]
            if chunk == chunks - 1:
                for part in range(parts):
                    begin = (chunk * parts + part) * HOP
                    carry(begin, begin + HOP, before=arrivals[part])
            else:
                carry(
                    chunk * LANES, (chunk + 1) * LANES,
                    before=lambda: [arrival() for arrival in arrivals],
                )
            carry_requests(chunk, last=True)
            finish_requests(chunk)
        for piece in range(PIECES):
            receive(piece)

    @pl.when(me == 0)
    def _():
        for chunk in range(chunks):
            carry(chunk * LANES, (chunk + 1) * LANES, alone=True)

    @pl.when(second & (core == 1))
    def _():
        for piece in range(PIECES):
            give(piece)

    def collect(q):
        @pl.when(q > me)
        def _():
            slots_from(q, lambda s: z_to(me, q, s).wait_recv())
            for chunk in range(chunks):
                add_z(zin, q, chunk)

    each(n, collect)

    @pl.when((me == 0) & (core == 1))
    def _():
        for piece in range(PIECES):
            give(piece)


    @pl.when(middle)
    def _():
        for piece in range(PIECES):
            receive(piece)

    done = jnp.where(present, res[...], 0.0).astype(BF16)
    for s in range(n):
        dout_ref[0, s] = done[s * STEPS:(s + 1) * STEPS]

    @pl.when(me < n - 1)
    def _():
        for hop in range(hops):
            onward(hop).wait_send()

    def finish(q):
        @pl.when(q != me)
        def _():
            query_slots(q, me, lambda copy: copy.wait_send())

        @pl.when(q < me)
        def _():
            log_to(q, me).wait_send()
            slots_from(me, lambda s: z_to(q, me, s).wait_send())

        @pl.when(q > me)
        def _():
            for piece in range(PIECES):
                r_to(q, me, piece).wait_send()

    each(n, finish)


def store(out_vmem, dout_vmem, out_hbm, dout_hbm, sem):
    copies = [
        pltpu.make_async_copy(out_vmem, out_hbm, sem.at[0]),
        pltpu.make_async_copy(dout_vmem, dout_hbm, sem.at[1]),
    ]
    for copy in copies:
        copy.start()
    for copy in copies:
        copy.wait()


def shards(
    ssm_input, bmat, cmat, dt_raw, a_log, d_skip, prompt_len, owner, dec_x, dec_b, dec_c, dec_dt
):
    n = lax.axis_size("seq")
    tokens, width = ssm_input.shape
    heads = dt_raw.shape[1]
    gn = bmat.shape[1]
    spans = tokens // SPAN
    hops = width // HOP
    rows = n * STEPS
    requests = prompt_len.shape[0]
    hbm = pl.BlockSpec(memory_space=pltpu.HBM)
    vmem = pl.BlockSpec(memory_space=pltpu.VMEM)
    dma = pltpu.SemaphoreType.DMA
    slots = (n, STEPS)
    operands = (
        ssm_input, bmat, cmat, dt_raw.T, a_log[None, :], d_skip[None, :],
        prompt_len[None, :], owner[None, :], dec_x, dec_b, dec_c, dec_dt,
    )
    out, dout = pl.pallas_call(
        functools.partial(kernel, n),
        out_shape=(
            pltpu.VMEM((tokens, width), BF16),
            pltpu.VMEM((1,) + slots + (width,), BF16),
        ),
        in_specs=[hbm] * 12,
        out_specs=(vmem, vmem),
        scratch_shapes=[
            pltpu.VMEM((tokens, width), BF16),
            pltpu.VMEM((tokens, gn), BF16),
            pltpu.VMEM((tokens, gn), BF16),
            pltpu.VMEM((heads, tokens), BF16),
            pltpu.VMEM((1, heads), F32),
            pltpu.VMEM((1, heads), F32),
            pltpu.VMEM((1, requests), jnp.int32),
            pltpu.VMEM((1, requests), jnp.int32),
            pltpu.VMEM(slots + (width,), BF16),
            pltpu.VMEM(slots + (gn,), BF16),
            pltpu.VMEM(slots + (heads,), BF16),
            pltpu.VMEM((n,) + slots + (gn,), BF16),
            pltpu.VMEM((rows, width), F32),
            pltpu.VMEM((rows, gn), F32),
            pltpu.VMEM((rows, heads), F32),
            pltpu.VMEM((rows, gn), F32),
            pltpu.VMEM((rows, gn), F32),
            pltpu.VMEM((n * rows, gn), F32),
            pltpu.VMEM((heads, width), BF16),
            pltpu.VMEM((8, width), F32),
            pltpu.VMEM((max(spans - 1, 1), N, width), F32),
            pltpu.VMEM((N, width), F32),
            pltpu.VMEM((tokens, width), F32),
            pltpu.VMEM((hops, N, HOP), BF16),
            pltpu.VMEM((hops, N, HOP), BF16),
            pltpu.VMEM((rows, width), F32),
            pltpu.VMEM((rows, width), F32),
            pltpu.VMEM((rows, width), F32),
            pltpu.VMEM((rows, width), F32),
            pltpu.VMEM((rows, width), F32),
            pltpu.VMEM((n,) + slots + (width,), BF16),
            pltpu.VMEM((n,) + slots + (width,), BF16),
            pltpu.VMEM((PIECES, n, STEPS, width // PIECES), BF16),
            pltpu.VMEM((PIECES, n, STEPS, width // PIECES), BF16),
            pltpu.VMEM((n, 8, heads), F32),
            pltpu.VMEM((n, 8, heads), F32),
            pltpu.VMEM((n + 2, 2, rows, heads), BF16),
            dma((15,)),
            dma((hops,)),
            dma((hops,)),
            dma((n, n if n <= FEW else 1)),
            dma((n, n if n <= FEW else 1)),
            dma((n,)),
            dma((n,)),
            dma((n, n)),
            dma((n, n)),
            dma((PIECES, n)),
            dma((PIECES, n)),
            pltpu.SemaphoreType.REGULAR((n,)),
        ],
        compiler_params=pltpu.CompilerParams(
            collective_id=0, has_side_effects=True, vmem_limit_bytes=61 * 1024 * 1024
        ),
    )(*(pltpu.with_memory_space_constraint(operand, pltpu.HBM) for operand in operands))
    return pl.pallas_call(
        store,
        out_shape=(
            jax.ShapeDtypeStruct(out.shape, BF16),
            jax.ShapeDtypeStruct(dout.shape, BF16),
        ),
        in_specs=[vmem, vmem],
        out_specs=(hbm, hbm),
        scratch_shapes=[dma((2,))],
    )(
        pltpu.with_memory_space_constraint(out, pltpu.VMEM),
        pltpu.with_memory_space_constraint(dout, pltpu.VMEM),
    )


def solution(mesh):
    placed = (
        P(("grp", "seq"), "tp"),
        P(("grp", "seq"), "tp"),
        P(("grp", "seq"), "tp"),
        P(("grp", "seq"), "tp"),
        P("tp"),
        P("tp"),
        P("grp"),
        P("grp"),
        P(("grp", "seq"), None, None, "tp"),
        P(("grp", "seq"), None, None, "tp"),
        P(("grp", "seq"), None, None, "tp"),
        P(("grp", "seq"), None, None, "tp"),
    )
    return jax.shard_map(
        shards,
        mesh=mesh,
        in_specs=placed,
        out_specs=(P(("grp", "seq"), "tp"), P(("grp", "seq"), None, None, "tp")),
        check_vma=False,
    )
```
